512 devices in a mesh: dp: 128 (over z, x, core), mp: 4 (over y).
Axes of the slice: x: 4, y: 4, z: 16, core: 2. Of those that a mesh axis runs over, the one named last changes fastest.
Arguments:
- patches: bfloat16 [131072, 1408], P('dp', 'mp'), may hold values from -6 to 6
- counts: int32 [128, 4, 4], P('dp'), may hold values from 32 to 64, as said below
- qkv_weight: bfloat16 [1408, 2112], P(None, 'mp')
- grad_context: bfloat16 [131072, 704], P('dp', 'mp'), may hold values from -6 to 6
Outputs:
- grad_patches: bfloat16 [131072, 1408], P('dp', 'mp')
- grad_weight: bfloat16 [1408, 2112], P(None, 'mp')
The draws below stay inside these ranges and needn't reach their ends.
Inputs may be any that keep to these rules, and one draw needn't show every extreme that they name: `counts`: in every draw one bundle holds 4 images of 64 patches, so a bundle's images fill at most 256 slots.
All inputs are finite; a program needn't handle non-finite values.
Results may differ from the reference program's by a relative error of at most 0.0065.
The reference program's roundings to bfloat16 on the way count: a program that leaves them out, or rounds other values in their place, can miss the bound.
Values may be sent and summed in bfloat16 or wider, within the bound.
A program may use at most 64 MiB of HBM per device.

```python
import math
from functools import partial
import jax
import jax.numpy as jnp
from jax import lax

D = 1408
HD = 88
HEADS = 8
MAXP = 64
MINP = 32
IMGS = 4
BUNDLES = 4
CAP = 256
SEQ = 1024
OWNERS = 128
N_DP = 128


def draw_counts(key, part):
    base = jax.random.randint(key, (OWNERS, BUNDLES, IMGS), MINP, MAXP + 1)
    chosen = jax.random.randint(jax.random.fold_in(key, 7), (), 0, OWNERS * BUNDLES)
    flat = jnp.arange(OWNERS * BUNDLES, dtype=jnp.int32).reshape(OWNERS, BUNDLES, 1)
    return jnp.where(flat == chosen, MAXP, base).astype(jnp.int32)


def draw_qkv_weight(key, part):
    raw = jax.random.normal(key, (D, HEADS * 3 * HD), jnp.float32) * (1.0 / math.sqrt(D))
    return raw.astype(jnp.bfloat16)


def shard_levels(key, extent, pieces, low, largest):
    def one(dim, shards_of):
        draws = jax.random.uniform(jax.random.fold_in(jax.random.fold_in(key, 6), dim), (shards_of,), jnp.float32, low / len(pieces), largest / len(pieces))
        return jnp.repeat(jnp.exp(draws), extent[dim] // shards_of).reshape((-1,) + (1,) * (len(extent) - dim - 1))

    gain = one(*pieces[0])
    for cut in pieces[1:]:
        gain = gain * one(*cut)
    return gain


def scatter_about(key, dims, deviation, most, shards=(), kind=jnp.bfloat16):
    gain = shard_levels(key, dims, shards, -0.22, 0.18) if shards else 1.0
    result = jax.random.normal(key, dims, jnp.float32) * deviation * gain
    return jnp.minimum(jnp.maximum(result, -most), most).astype(kind)


def setup_inputs(seed: int = 0) -> dict:
    seeds = jax.random.split(jax.random.key(seed), 5)
    return {
        "patches": scatter_about(seeds[0], (OWNERS * SEQ, D), 1.0, 6.0, ((0, 128), (1, 4))),
        "counts": draw_counts(jax.random.fold_in(seeds[4], 71), 0),
        "qkv_weight": draw_qkv_weight(jax.random.fold_in(seeds[4], 71), 0),
        "grad_context": scatter_about(seeds[3], (OWNERS * SEQ, HEADS * HD), 1.0, 6.0, ((0, 128), (1, 4))),
    }


def layout(counts_here):
    image_ends = jnp.cumsum(counts_here, axis=1).astype(jnp.int32)
    position = jnp.arange(CAP, dtype=jnp.int32)
    segment = lax.optimization_barrier(jnp.sum((position[None, :, None] >= image_ends[:, None, :]).astype(jnp.int32), axis=2))
    is_valid = segment < IMGS
    same_image = segment[:, :, None] == segment[:, None, :]
    diagonal = position[:, None] == position[None, :]
    allowed = jnp.where(is_valid[:, :, None], same_image, diagonal[None])
    return (is_valid, allowed)

def shift_list():
    stride = N_DP // BUNDLES
    return [stride // 2 + bundle * stride for bundle in range(BUNDLES)]

def one_sequence(weight, total, items):
    seq_rows, counts_here, upstream_rows = items
    width = 3 * HEADS * HD
    packed = jnp.dot(seq_rows, weight, preferred_element_type=jnp.float32).astype(jnp.bfloat16)
    packed = packed.reshape(BUNDLES, CAP, HEADS, 3, HD)
    queries = packed[:, :, :, 0].astype(jnp.float32)
    key_rows = packed[:, :, :, 1].astype(jnp.float32)
    value_rows = packed[:, :, :, 2].astype(jnp.float32)
    is_valid, allowed = layout(counts_here)
    scale = 1.0 / math.sqrt(HD)
    scores = jnp.einsum('bqhd,bkhd->bhqk', queries, key_rows) * scale
    masked = jnp.where(allowed[:, None], scores, -1e+30)
    top = lax.optimization_barrier(jnp.max(masked, axis=-1, keepdims=True))
    exponent = jnp.where(allowed[:, None], jnp.exp(masked - top), 0.0)
    attn_probs = exponent / lax.optimization_barrier(jnp.sum(exponent, axis=-1, keepdims=True))
    probs_low = attn_probs.astype(jnp.bfloat16).astype(jnp.float32)
    upstream = upstream_rows.reshape(BUNDLES, CAP, HEADS, HD) * is_valid[:, :, None, None].astype(jnp.bfloat16)
    upstream = upstream.astype(jnp.float32)
    grad_probs = jnp.einsum('bqhd,bkhd->bhqk', upstream, value_rows)
    grad_values = jnp.einsum('bhqk,bqhd->bkhd', probs_low, upstream).astype(jnp.bfloat16)
    row_dot = lax.optimization_barrier(jnp.sum(attn_probs * grad_probs, axis=-1, keepdims=True))
    grad_logits = (attn_probs * (grad_probs - row_dot) * scale).astype(jnp.bfloat16).astype(jnp.float32)
    grad_queries = jnp.einsum('bhqk,bkhd->bqhd', grad_logits, key_rows).astype(jnp.bfloat16)
    grad_keys = jnp.einsum('bhqk,bqhd->bkhd', grad_logits, queries).astype(jnp.bfloat16)
    grad_packed = jnp.stack([grad_queries, grad_keys, grad_values], axis=3).reshape(SEQ, width)
    weight_term = jnp.dot(seq_rows.T, grad_packed, preferred_element_type=jnp.float32)
    grad_rows = jnp.dot(grad_packed, weight.T, preferred_element_type=jnp.float32).astype(jnp.bfloat16)
    return (total + weight_term, grad_rows)

def reference(patches, counts, qkv_weight, grad_context):
    shifts = shift_list()
    source = patches.reshape(N_DP, BUNDLES, CAP, D)
    seq_all = jnp.stack([jnp.roll(source[:, bundle], -shifts[bundle], axis=0) for bundle in range(BUNDLES)], axis=1)
    seq_all = seq_all.reshape(N_DP, SEQ, D)
    upstream_all = grad_context.reshape(N_DP, SEQ, HEADS * HD)
    start = jnp.zeros((D, 3 * HEADS * HD), jnp.float32)
    total, grad_seq = lax.scan(partial(one_sequence, qkv_weight), start, (seq_all, counts, upstream_all))
    grad_weight = (total / math.sqrt(N_DP)).astype(jnp.bfloat16)
    grad_seq = grad_seq.reshape(N_DP, BUNDLES, CAP, D)
    grad_patches = jnp.stack([jnp.roll(grad_seq[:, bundle], shifts[bundle], axis=0) for bundle in range(BUNDLES)], axis=1)
    return (grad_patches.reshape(N_DP * SEQ, D), grad_weight)
```

```python
import functools
import math

import jax
import jax.numpy as jnp
from jax import lax
from jax.experimental import pallas as pl
from jax.experimental.pallas import tpu as pltpu
from jax.sharding import PartitionSpec as P

HD = 88
IMGS = 4
BUNDLES = 4
CAP = 256
SEQ = 1024
YS = 4
XS = 4
CORES = 2
LANES = 128
GROW = 192

F32 = jnp.float32
BF16 = jnp.bfloat16


def dot(a, b, dims):
    return lax.dot_general(a, b, (dims, ((), ())), preferred_element_type=F32)


def routed_rows(counts_here, grad_context):
    ends = jnp.cumsum(counts_here, axis=1)
    position = jnp.arange(CAP, dtype=jnp.int32)
    segment = jnp.sum((position[None, :, None] >= ends[:, None, :]).astype(jnp.int32), axis=2)
    is_valid = segment < IMGS
    ids = jnp.where(is_valid, segment - IMGS, position[None]).astype(BF16)
    heads = grad_context.shape[1] // HD
    up = grad_context.reshape(BUNDLES, CAP, heads, HD) * is_valid[:, :, None, None].astype(BF16)
    up = up.transpose(0, 2, 3, 1)
    tags = jnp.broadcast_to(ids[:, None, None, :], (BUNDLES, heads, 8, CAP))
    return jnp.concatenate([up, tags], axis=2).reshape(BUNDLES, heads * (HD + 8), CAP)


def kernel(
    n_dp,
    x_hbm, g_hbm, w_hbm,
    gx_hbm, fin_hbm,
    xs, big_x, wv, wt, gb, pk, gps, gp, wfb, wf, dw, c0, ra1, ra2, rb1, rb2, ze, zr, fin, gxv,
    x_ss, x_rs, g_ss, g_rs, p_ss, p_rs, w_ss, w_rs, v_ss, v_rs, d_ss, d_rs, z_ss, z_rs, f_ss, f_rs, l_sem, o_sem,
):
    feat = x_hbm.shape[1]
    width = w_hbm.shape[1]
    heads = width // (3 * HD)
    d_model = YS * feat
    nz = n_dp // (XS * CORES)
    stride = n_dp // BUNDLES
    scale = 1.0 / math.sqrt(HD)
    norm = 1.0 / math.sqrt(n_dp)
    half = fin.shape[0] // 2
    sub = half // 2
    q1 = sub // 2
    q2 = q1 // 2
    piece = 2 * q2 // nz

    dp = lax.axis_index("dp")
    me = lax.axis_index("mp")
    right, left, far = (me + 1) % YS, (me + 3) % YS, (me + 2) % YS
    core = dp % CORES
    xi = (dp // CORES) % XS
    zi = dp // (XS * CORES)
    base_xz = zi * (XS * CORES)
    mate = {"dp": dp + 1 - 2 * core}
    even = xi % 2
    near1 = {"dp": base_xz + (xi + 1 - 2 * even) * CORES + core}
    near2 = {"dp": base_xz + ((xi + 3 - 2 * even) % XS) * CORES + core}
    bit1 = ((xi + 1) // 2) % 2
    bit2 = xi // 2

    def z_peer(k):
        return {"dp": ((zi + k) % nz) * (XS * CORES) + xi * CORES + core}

    def remote(src, dst, ss, rs, dev):
        return pltpu.make_async_remote_copy(
            src_ref=src, dst_ref=dst, send_sem=ss, recv_sem=rs,
            device_id=dev, device_id_type=pl.DeviceIdType.MESH,
        )

    def rows(start, size):
        return pl.ds(pl.multiple_of(start, 16), size)

    def order(i):
        return (3 * i) % BUNDLES

    def g_copy(b):
        off = stride // 2 + b * stride
        return remote(g_hbm.at[b], gb.at[b], g_ss.at[b], g_rs.at[b], {"dp": (dp + off) % n_dp})

    def x_copies(b):
        r = rows(b * CAP, CAP)
        return (
            remote(x_hbm.at[r], xs.at[me, r], x_ss.at[0, b], x_rs.at[0, b], {"mp": right}),
            remote(x_hbm.at[r], xs.at[me, r], x_ss.at[1, b], x_rs.at[1, b], {"mp": left}),
        )

    def x_relays(b):
        r = rows(b * CAP, CAP // 2)
        s = rows(b * CAP + CAP // 2, CAP // 2)
        return (
            remote(xs.at[left, r], xs.at[left, r], x_ss.at[2, b], x_rs.at[2, b], {"mp": right}),
            remote(xs.at[right, s], xs.at[right, s], x_ss.at[3, b], x_rs.at[3, b], {"mp": left}),
        )

    def p_copies(b):
        r = rows(me * width, width)
        return (
            remote(gp.at[b, r], gp.at[b, r], p_ss.at[0, b], p_rs.at[0, b], {"mp": right}),
            remote(gp.at[b, r], gp.at[b, r], p_ss.at[1, b], p_rs.at[1, b], {"mp": left}),
        )

    def p_relays(b):
        r = rows(left * width, 256)
        s = rows(right * width + 256, width - 256)
        return (
            remote(gp.at[b, r], gp.at[b, r], p_ss.at[2, b], p_rs.at[2, b], {"mp": right}),
            remote(gp.at[b, s], gp.at[b, s], p_ss.at[3, b], p_rs.at[3, b], {"mp": left}),
        )

    fh = feat // CORES

    def w_copy(k):
        to = (me + k) % YS
        return remote(
            w_hbm.at[rows(to * feat + core * fh, fh)], wfb.at[me, rows(core * fh, fh)],
            w_ss.at[k - 1], w_rs.at[k - 1], {"mp": to},
        )

    def v_copy(k):
        who = (me + YS - k) % YS
        r = rows(core * fh, fh)
        return remote(wfb.at[who, r], wfb.at[who, r], v_ss.at[k - 1], v_rs.at[k - 1], mate)

    own = core * half
    oa, ob = own, own + sub
    keep_a, keep_b = oa + bit1 * q1, ob + bit2 * q1
    fa, fb = keep_a + bit2 * q2, keep_b + bit1 * q2
    core_rs = remote(dw.at[rows((1 - core) * half, half)], c0, d_ss.at[0], d_rs.at[0], mate)
    a1 = remote(dw.at[rows(oa + (1 - bit1) * q1, q1)], ra1, d_ss.at[1], d_rs.at[1], near1)
    b1 = remote(dw.at[rows(ob + (1 - bit2) * q1, q1)], rb1, d_ss.at[2], d_rs.at[2], near2)
    give_a2, give_b2 = keep_a + (1 - bit2) * q2, keep_b + (1 - bit1) * q2
    a2 = remote(dw.at[rows(give_a2, q2)], ra2, d_ss.at[3], d_rs.at[3], near2)
    b2 = remote(dw.at[rows(give_b2, q2)], rb2, d_ss.at[4], d_rs.at[4], near1)

    def z_copy(k):
        to = (zi + k) % nz
        return remote(ze.at[rows(to * piece, piece)], zr.at[k], z_ss.at[k], z_rs.at[k], z_peer(k))

    def spot(z):
        return jnp.where(z < nz // 2, fa + z * piece, fb + (z - nz // 2) * piece)

    def f_copy(k):
        r = rows(spot(zi), piece)
        return remote(fin.at[r], fin.at[r], f_ss.at[k], f_rs.at[k], z_peer(k))

    def same(start, size, i, dev):
        r = rows(start, size)
        return remote(fin.at[r], fin.at[r], d_ss.at[i], d_rs.at[i], dev)

    ag_a2, ag_b2 = same(fa, q2, 5, near2), same(fb, q2, 6, near1)
    ag_a1, ag_b1 = same(keep_a, q1, 7, near1), same(keep_b, q1, 8, near2)
    ag_core = same(own, half, 9, mate)

    barrier = pltpu.get_barrier_semaphore()
    mesh_id = pl.DeviceIdType.MESH
    for dev in [{"mp": right}, {"mp": left}, {"mp": far}, mate, near1, near2]:
        pl.semaphore_signal(barrier, inc=1, device_id=dev, device_id_type=mesh_id)

    def greet(k, _):
        pl.semaphore_signal(barrier, inc=1, device_id=z_peer(k), device_id_type=mesh_id)
        return 0

    lax.fori_loop(1, nz, greet, 0)
    pl.semaphore_wait(barrier, 6 + nz - 1)

    def start(copies):
        for cp in copies:
            cp.start()

    def arrive(copies):
        for cp in copies:
            cp.wait_recv()

    start(x_copies(0))
    for i in range(BUNDLES):
        g_copy(order(i)).start()
    start(x_copies(order(1)))
    w_local = pltpu.make_async_copy(w_hbm, wv, l_sem.at[0])
    w_local.start()
    x_local = pltpu.make_async_copy(x_hbm, xs.at[me], l_sem.at[1])
    x_local.start()
    wf_local = pltpu.make_async_copy(w_hbm.at[rows(me * feat, feat)], wfb.at[me], l_sem.at[2])
    wf_local.start()

    big_x[:, d_model:] = jnp.zeros((SEQ, big_x.shape[1] - d_model), BF16)
    w_local.wait()
    for n in range(d_model // LANES):
        wt[:, n * LANES:(n + 1) * LANES] = wv[n * LANES:(n + 1) * LANES, :].T
    x_local.wait()

    arrive(x_copies(0))
    start(x_relays(0))
    start(x_copies(order(2)))

    def bundle(i, _):
        b = order(i)

        @pl.when(i < BUNDLES - 1)
        def _():
            nxt = order(i + 1)
            arrive(x_copies(nxt))
            start(x_relays(nxt))

        @pl.when(i == 0)
        def _():
            start(x_copies(order(3)))

        @pl.when(i == 2)
        def _():
            for k in range(1, YS):
                w_copy(k).start()
            start(p_copies(order(0)))
            start(p_copies(order(1)))

        @pl.when(i == 3)
        def _():
            start(p_copies(order(2)))

        arrive(x_relays(b))
        r = rows(b * CAP, CAP)
        for j in range(YS):
            big_x[r, j * feat:(j + 1) * feat] = xs[j, r, :]
        pk[...] = dot(wt[...], big_x[r, :d_model], ((1,), (1,)))
        g_copy(b).wait_recv()
        tags = gb[b, GROW // 2 - 16:GROW // 2, :].astype(F32)[8:16]
        allowed = tags[0:1, :] == tags.T[:, 0:1]
        for h in range(heads):
            o = h * 3 * HD
            query = pk[o:o + HD, :].astype(BF16)
            key = pk[o + HD:o + 2 * HD, :].astype(BF16)
            value = pk[o + 2 * HD:o + 3 * HD, :].astype(BF16)
            up = gb[b, h * (HD + 8):h * (HD + 8) + HD, :]
            scores = dot(query, key, ((0,), (0,))) * scale
            masked = jnp.where(allowed, scores, -1e30)
            top = jnp.max(masked, axis=1, keepdims=True)
            exponent = jnp.where(allowed, jnp.exp(masked - top), 0.0)
            probs = exponent * (1.0 / jnp.sum(exponent, axis=1, keepdims=True))
            grad_probs = dot(up, value, ((0,), (0,)))
            row_dot = jnp.sum(probs * grad_probs, axis=1, keepdims=True)
            logits = (probs * (grad_probs - row_dot) * scale).astype(BF16)
            gps[o:o + HD, :] = dot(key, logits, ((1,), (1,)))
            gps[o + HD:o + 2 * HD, :] = dot(query, logits, ((1,), (0,)))
            gps[o + 2 * HD:o + 3 * HD, :] = dot(up, probs.astype(BF16), ((1,), (0,)))
        gp[b, rows(me * width, width), :] = gps[...].astype(BF16)
        return 0

    lax.fori_loop(0, BUNDLES, bundle, 0)
    start(p_copies(order(3)))

    mine = rows(me * width, width)

    def weight_block(n, _):
        cols = pl.ds(pl.multiple_of(n * 2 * LANES, 2 * LANES), 2 * LANES)
        total = dot(gp[0, mine, :], big_x[0:CAP, cols], ((1,), (0,)))
        for b in range(1, BUNDLES):
            total += dot(gp[b, mine, :], big_x[b * CAP:(b + 1) * CAP, cols], ((1,), (0,)))
        at = n * 2 * width
        dw[rows(at, width), :] = total[:, :LANES]
        dw[rows(at + width, width), :] = total[:, LANES:]
        return 0

    lax.fori_loop(0, big_x.shape[1] // (2 * LANES), weight_block, 0)
    core_rs.start()

    for k in range(1, YS):
        w_copy(k).wait_recv()
        v_copy(k).start()
    core_rs.wait_recv()

    def add_core(n, _):
        r = rows(own + n * q2, q2)
        dw[r, :] += c0[rows(n * q2, q2), :]
        return 0

    lax.fori_loop(0, half // q2, add_core, 0)
    a1.start()
    b1.start()

    wf_local.wait()
    for k in range(1, YS):
        v_copy(k).wait_recv()
    for j in range(YS):
        wf[:, j * width:(j + 1) * width] = wfb[j]

    a1.wait_recv()
    b1.wait_recv()

    def add_into(at, got, got_at, size):
        dw[rows(at, size), :] += got[rows(got_at, size), :]

    add_into(give_a2, ra1, (1 - bit2) * q2, q2)
    add_into(give_b2, rb1, (1 - bit1) * q2, q2)
    a2.start()
    b2.start()
    add_into(fa, ra1, bit2 * q2, q2)
    add_into(fb, rb1, bit1 * q2, q2)

    for i in range(2):
        arrive(p_copies(order(i)))
        start(p_relays(order(i)))

    a2.wait_recv()
    b2.wait_recv()
    ze[0:q2, :] = dw[rows(fa, q2), :] + ra2[...]
    ze[q2:2 * q2, :] = dw[rows(fb, q2), :] + rb2[...]

    def loop_z(f):
        def body(k, _):
            f(k)
            return 0

        lax.fori_loop(1, nz, body, 0)

    loop_z(lambda k: z_copy(k).start())

    for i in range(2, BUNDLES):
        arrive(p_copies(order(i)))
        start(p_relays(order(i)))

    def gx_copy(b):
        return pltpu.make_async_copy(gxv.at[b], gx_hbm.at[b], o_sem.at[b])

    def rows_grad(i, _):
        b = order(i)
        arrive(p_relays(b))
        gxv[b] = dot(wf[...], gp[b], ((1,), (0,))).astype(BF16)
        gx_copy(b).start()
        return 0

    lax.fori_loop(0, BUNDLES, rows_grad, 0)

    loop_z(lambda k: z_copy(k).wait_recv())

    def add_z(k, total):
        return total + zr[k]

    total = lax.fori_loop(1, nz, add_z, ze[rows(zi * piece, piece), :])
    fin[rows(spot(zi), piece), :] = (total * norm).astype(BF16)
    loop_z(lambda k: f_copy(k).start())
    loop_z(lambda k: f_copy(k).wait_recv())
    ag_a2.start()
    ag_b2.start()
    ag_a2.wait_recv()
    ag_b2.wait_recv()
    ag_a1.start()
    ag_b1.start()
    ag_a1.wait_recv()
    ag_b1.wait_recv()
    ag_core.start()
    mine_out = pltpu.make_async_copy(
        fin.at[rows(own, half)], fin_hbm.at[rows(own, half)], o_sem.at[BUNDLES])
    mine_out.start()
    ag_core.wait_recv()
    rest_out = pltpu.make_async_copy(
        fin.at[rows((1 - core) * half, half)], fin_hbm.at[rows((1 - core) * half, half)],
        o_sem.at[BUNDLES + 1])
    rest_out.start()

    for b in range(BUNDLES):
        g_copy(b).wait_send()
        for cp in x_copies(b) + x_relays(b) + p_copies(b) + p_relays(b):
            cp.wait_send()
        gx_copy(b).wait()
    for k in range(1, YS):
        w_copy(k).wait_send()
        v_copy(k).wait_send()
    for cp in (core_rs, a1, b1, a2, b2, ag_a2, ag_b2, ag_a1, ag_b1, ag_core):
        cp.wait_send()
    loop_z(lambda k: z_copy(k).wait_send())
    loop_z(lambda k: f_copy(k).wait_send())
    mine_out.wait()
    rest_out.wait()


def shards(patches, counts, qkv_weight, grad_context):
    n_dp = lax.axis_size("dp")
    nz = n_dp // (XS * CORES)
    feat = patches.shape[1]
    width = qkv_weight.shape[1]
    d_model = YS * feat
    blocks = d_model // LANES
    parts = n_dp
    unit = -(-(blocks * width) // (parts * 16)) * 16
    flat = unit * parts
    wide = 2 * LANES * (-(-blocks // 2))
    half = flat // 2
    q1, q2 = half // 4, half // 8
    routed = routed_rows(counts[0], grad_context)
    dma = pltpu.SemaphoreType.DMA
    any_spec = pl.BlockSpec(memory_space=pl.ANY)
    gx, fin = pl.pallas_call(
        functools.partial(kernel, n_dp),
        out_shape=(
            jax.ShapeDtypeStruct((BUNDLES, feat, CAP), BF16),
            jax.ShapeDtypeStruct((flat, LANES), BF16),
        ),
        in_specs=[any_spec] * 3,
        out_specs=(any_spec, any_spec),
        scratch_shapes=[
            pltpu.VMEM((YS, SEQ, feat), BF16),
            pltpu.VMEM((SEQ, wide), BF16),
            pltpu.VMEM((d_model, width), BF16),
            pltpu.VMEM((width, d_model), BF16),
            pltpu.VMEM((BUNDLES, GROW, CAP), BF16),
            pltpu.VMEM((width, CAP), F32),
            pltpu.VMEM((width, CAP), F32),
            pltpu.VMEM((BUNDLES, YS * width, CAP), BF16),
            pltpu.VMEM((YS, feat, width), BF16),
            pltpu.VMEM((feat, YS * width), BF16),
            pltpu.VMEM((max(flat, wide // LANES * width), LANES), F32),
            pltpu.VMEM((half, LANES), F32),
            pltpu.VMEM((q1, LANES), F32),
            pltpu.VMEM((q2, LANES), F32),
            pltpu.VMEM((q1, LANES), F32),
            pltpu.VMEM((q2, LANES), F32),
            pltpu.VMEM((2 * q2, LANES), F32),
            pltpu.VMEM((nz, 2 * q2 // nz, LANES), F32),
            pltpu.VMEM((flat, LANES), BF16),
            pltpu.VMEM((BUNDLES, feat, CAP), BF16),
            dma((4, BUNDLES)), dma((4, BUNDLES)),
            dma((BUNDLES,)), dma((BUNDLES,)),
            dma((4, BUNDLES)), dma((4, BUNDLES)),
            dma((YS - 1,)), dma((YS - 1,)),
            dma((YS - 1,)), dma((YS - 1,)),
            dma((10,)), dma((10,)),
            dma((nz,)), dma((nz,)),
            dma((nz,)), dma((nz,)),
            dma((3,)), dma((BUNDLES + 2,)),
        ],
        compiler_params=pltpu.CompilerParams(
            collective_id=0, has_side_effects=True, vmem_limit_bytes=60 * 1024 * 1024),
        name="layer",
    )(patches, routed, qkv_weight)
    grad_patches = gx.transpose(0, 2, 1).reshape(SEQ, feat)
    grad_weight = fin[:blocks * width].reshape(blocks, width, LANES).transpose(0, 2, 1)
    return grad_patches, grad_weight.reshape(d_model, width)


def solution(mesh):
    in_specs = (P("dp", "mp"), P("dp", None, None), P(None, "mp"), P("dp", "mp"))
    out_specs = (P("dp", "mp"), P(None, "mp"))
    return jax.shard_map(shards, mesh=mesh, in_specs=in_specs, out_specs=out_specs, check_vma=False)
```

```python
import functools
import math

import jax
import jax.numpy as jnp
from jax import lax
from jax.experimental import pallas as pl
from jax.experimental.pallas import tpu as pltpu
from jax.sharding import PartitionSpec as P

HD = 88
IMGS = 4
BUNDLES = 4
CAP = 256
SEQ = 1024
YS = 4
XS = 4
CORES = 2
LANES = 128
TAG = 16

F32 = jnp.float32
BF16 = jnp.bfloat16


def dot(a, b, dims):
    return lax.dot_general(a, b, (dims, ((), ())), preferred_element_type=F32)


def kernel(
    n_dp,
    x_hbm, g_hbm, w_hbm, counts,
    gx_hbm, fin_hbm,
    xt, wt, wn, tag, gt, gb, pk, up_all, gps, gp, wfb, wf, dw, c0, ra1, ra2, rb1, rb2, ze, zr, fin, gxv,
    x_ss, x_rs, g_ss, g_rs, t_ss, t_rs, p_ss, p_rs, w_ss, w_rs, v_ss, v_rs, d_ss, d_rs, z_ss, z_rs, f_ss, f_rs, l_sem, o_sem,
):
    feat = x_hbm.shape[0]
    width = w_hbm.shape[0]
    heads = width // (3 * HD)
    d_model = YS * feat
    nz = n_dp // (XS * CORES)
    stride = n_dp // BUNDLES
    scale = 1.0 / math.sqrt(HD)
    norm = 1.0 / math.sqrt(n_dp)
    half = fin.shape[0] // 2
    sub = half // 2
    q1 = sub // 2
    q2 = q1 // 2
    piece = 2 * q2 // nz

    dp = lax.axis_index("dp")
    me = lax.axis_index("mp")
    right, left, far = (me + 1) % YS, (me + 3) % YS, (me + 2) % YS
    core = dp % CORES
    xi = (dp // CORES) % XS
    zi = dp // (XS * CORES)
    base_xz = zi * (XS * CORES)
    mate = {"dp": dp + 1 - 2 * core}
    even = xi % 2
    near1 = {"dp": base_xz + (xi + 1 - 2 * even) * CORES + core}
    near2 = {"dp": base_xz + ((xi + 3 - 2 * even) % XS) * CORES + core}
    bit1 = ((xi + 1) // 2) % 2
    bit2 = xi // 2

    def z_peer(k):
        return {"dp": ((zi + k) % nz) * (XS * CORES) + xi * CORES + core}

    def remote(src, dst, ss, rs, dev):
        return pltpu.make_async_remote_copy(
            src_ref=src, dst_ref=dst, send_sem=ss, recv_sem=rs,
            device_id=dev, device_id_type=pl.DeviceIdType.MESH,
        )

    def rows(start, size):
        return pl.ds(pl.multiple_of(start, 16), size)

    def order(i):
        return (3 * i) % BUNDLES

    def cols(b):
        return pl.ds(pl.multiple_of(b * CAP, CAP), CAP)

    def g_copy(b):
        off = stride // 2 + b * stride
        to = {"dp": (dp + off) % n_dp}
        return (
            remote(tag.at[b], gt.at[b], t_ss.at[b], t_rs.at[b], to),
            remote(g_hbm.at[:, cols(b)], gb.at[b], g_ss.at[b], g_rs.at[b], to),
        )

    def x_copies(b):
        src = x_hbm.at[:, cols(b)]
        r = rows(me * feat, feat)
        return (
            remote(src, xt.at[b, r], x_ss.at[0, b], x_rs.at[0, b], {"mp": right}),
            remote(src, xt.at[b, r], x_ss.at[1, b], x_rs.at[1, b], {"mp": left}),
        )

    def x_relays(b):
        r = rows(left * feat, feat // 2)
        s = rows(right * feat + feat // 2, feat // 2)
        return (
            remote(xt.at[b, r], xt.at[b, r], x_ss.at[2, b], x_rs.at[2, b], {"mp": right}),
            remote(xt.at[b, s], xt.at[b, s], x_ss.at[3, b], x_rs.at[3, b], {"mp": left}),
        )

    def x_local(b):
        return pltpu.make_async_copy(
            x_hbm.at[:, cols(b)], xt.at[b, rows(me * feat, feat)], l_sem.at[b])

    def p_copies(b):
        r = rows(me * width, width)
        return (
            remote(gp.at[b, r], gp.at[b, r], p_ss.at[0, b], p_rs.at[0, b], {"mp": right}),
            remote(gp.at[b, r], gp.at[b, r], p_ss.at[1, b], p_rs.at[1, b], {"mp": left}),
        )

    def p_relays(b):
        r = rows(left * width, 256)
        s = rows(right * width + 256, width - 256)
        return (
            remote(gp.at[b, r], gp.at[b, r], p_ss.at[2, b], p_rs.at[2, b], {"mp": right}),
            remote(gp.at[b, s], gp.at[b, s], p_ss.at[3, b], p_rs.at[3, b], {"mp": left}),
        )

    fh = feat // CORES

    def w_copy(k):
        to = (me + k) % YS
        return remote(
            wn.at[rows(to * feat + core * fh, fh)], wfb.at[me, rows(core * fh, fh)],
            w_ss.at[k - 1], w_rs.at[k - 1], {"mp": to},
        )

    def v_copy(k):
        who = (me + YS - k) % YS
        r = rows(core * fh, fh)
        return remote(wfb.at[who, r], wfb.at[who, r], v_ss.at[k - 1], v_rs.at[k - 1], mate)

    own = core * half
    oa, ob = own, own + sub
    keep_a, keep_b = oa + bit1 * q1, ob + bit2 * q1
    fa, fb = keep_a + bit2 * q2, keep_b + bit1 * q2
    core_rs = remote(dw.at[rows((1 - core) * half, half)], c0, d_ss.at[0], d_rs.at[0], mate)
    a1 = remote(dw.at[rows(oa + (1 - bit1) * q1, q1)], ra1, d_ss.at[1], d_rs.at[1], near1)
    b1 = remote(dw.at[rows(ob + (1 - bit2) * q1, q1)], rb1, d_ss.at[2], d_rs.at[2], near2)
    give_a2, give_b2 = keep_a + (1 - bit2) * q2, keep_b + (1 - bit1) * q2
    a2 = remote(dw.at[rows(give_a2, q2)], ra2, d_ss.at[3], d_rs.at[3], near2)
    b2 = remote(dw.at[rows(give_b2, q2)], rb2, d_ss.at[4], d_rs.at[4], near1)

    def z_copy(k):
        to = (zi + k) % nz
        return remote(ze.at[rows(to * piece, piece)], zr.at[k], z_ss.at[k], z_rs.at[k], z_peer(k))

    def spot(z):
        return jnp.where(z < nz // 2, fa + z * piece, fb + (z - nz // 2) * piece)

    def f_copy(k):
        r = rows(spot(zi), piece)
        return remote(fin.at[r], fin.at[r], f_ss.at[k], f_rs.at[k], z_peer(k))

    def same(start, size, i, dev):
        r = rows(start, size)
        return remote(fin.at[r], fin.at[r], d_ss.at[i], d_rs.at[i], dev)

    ag_a2, ag_b2 = same(fa, q2, 5, near2), same(fb, q2, 6, near1)
    ag_a1, ag_b1 = same(keep_a, q1, 7, near1), same(keep_b, q1, 8, near2)
    ag_core = same(own, half, 9, mate)

    barrier = pltpu.get_barrier_semaphore()
    mesh_id = pl.DeviceIdType.MESH

    def greet(k, _):
        pl.semaphore_signal(barrier, inc=1, device_id=z_peer(k), device_id_type=mesh_id)
        return 0

    lax.fori_loop(1, nz, greet, 0)
    for dev in [{"mp": right}, {"mp": left}, {"mp": far}, mate, near1, near2]:
        pl.semaphore_signal(barrier, inc=1, device_id=dev, device_id_type=mesh_id)
    w_local = pltpu.make_async_copy(w_hbm, wt, l_sem.at[BUNDLES])
    w_local.start()
    for i in range(BUNDLES):
        x_local(order(i)).start()

    slot = lax.broadcasted_iota(jnp.int32, (TAG, CAP), 1)
    for b in range(BUNDLES):
        end = counts[b, 0]
        ids = jnp.where(slot >= end, 1, 0)
        for i in range(1, IMGS):
            end = end + counts[b, i]
            ids = ids + jnp.where(slot >= end, 1, 0)
        tag[b] = jnp.where(slot < end, ids - IMGS, slot).astype(F32).astype(BF16)
    for b in range(BUNDLES):
        xt[b, d_model:, :] = jnp.zeros((xt.shape[1] - d_model, CAP), BF16)
    pl.semaphore_wait(barrier, 6 + nz - 1)

    def start(copies):
        for cp in copies:
            cp.start()

    def arrive(copies):
        for cp in copies:
            cp.wait_recv()

    start(x_copies(0))
    for i in range(BUNDLES):
        start(g_copy(order(i)))
    start(x_copies(order(1)))
    w_local.wait()
    for n in range(d_model // LANES):
        wn[n * LANES:(n + 1) * LANES, :] = wt[:, n * LANES:(n + 1) * LANES].T
    for i in range(BUNDLES):
        x_local(order(i)).wait()
    wfb[me] = wn[rows(me * feat, feat), :]

    arrive(x_copies(0))
    start(x_relays(0))
    start(x_copies(order(2)))

    def bundle(i, _):
        b = order(i)

        @pl.when(i < BUNDLES - 1)
        def _():
            nxt = order(i + 1)
            arrive(x_copies(nxt))
            start(x_relays(nxt))

        @pl.when(i == 0)
        def _():
            start(x_copies(order(3)))

        @pl.when(i == 2)
        def _():
            for k in range(1, YS):
                w_copy(k).start()
            start(p_copies(order(0)))
            start(p_copies(order(1)))

        @pl.when(i == 3)
        def _():
            start(p_copies(order(2)))

        arrive(x_relays(b))
        pk[...] = dot(wt[...], xt[b, 0:d_model, :], ((1,), (0,)))
        arrive(g_copy(b))
        tags = gt[b].astype(F32)[0:8]
        allowed = tags[0:1, :] == tags.T[:, 0:1]
        up_all[...] = jnp.where(tags[0:1, :] < 0, gb[b].astype(F32), 0.0)
        for h in range(heads):
            o = h * 3 * HD
            query = pk[o:o + HD, :].astype(BF16)
            key = pk[o + HD:o + 2 * HD, :].astype(BF16)
            value = pk[o + 2 * HD:o + 3 * HD, :].astype(BF16)
            up = up_all[h * HD:(h + 1) * HD, :].astype(BF16)
            scores = dot(query, key, ((0,), (0,))) * scale
            masked = jnp.where(allowed, scores, -1e30)
            top = jnp.max(masked, axis=1, keepdims=True)
            exponent = jnp.where(allowed, jnp.exp(masked - top), 0.0)
            probs = exponent * (1.0 / jnp.sum(exponent, axis=1, keepdims=True))
            grad_probs = dot(up, value, ((0,), (0,)))
            row_dot = jnp.sum(probs * grad_probs, axis=1, keepdims=True)
            logits = (probs * (grad_probs - row_dot) * scale).astype(BF16)
            gps[o:o + HD, :] = dot(key, logits, ((1,), (1,)))
            gps[o + HD:o + 2 * HD, :] = dot(query, logits, ((1,), (0,)))
            gps[o + 2 * HD:o + 3 * HD, :] = dot(up, probs.astype(BF16), ((1,), (0,)))
        gp[b, rows(me * width, width), :] = gps[...].astype(BF16)
        return 0

    lax.fori_loop(0, BUNDLES, bundle, 0)
    start(p_copies(order(3)))

    mine = rows(me * width, width)

    def weight_block(n, _):
        block = rows(n * 2 * LANES, 2 * LANES)
        total = dot(gp[0, mine, :], xt[0, block, :], ((1,), (1,)))
        for b in range(1, BUNDLES):
            total += dot(gp[b, mine, :], xt[b, block, :], ((1,), (1,)))
        at = n * 2 * width
        dw[rows(at, width), :] = total[:, :LANES]
        dw[rows(at + width, width), :] = total[:, LANES:]
        return 0

    lax.fori_loop(0, xt.shape[1] // (2 * LANES), weight_block, 0)
    core_rs.start()

    for k in range(1, YS):
        w_copy(k).wait_recv()
        v_copy(k).start()
    core_rs.wait_recv()

    def add_core(n, _):
        r = rows(own + n * q2, q2)
        dw[r, :] += c0[rows(n * q2, q2), :]
        return 0

    lax.fori_loop(0, half // q2, add_core, 0)
    a1.start()
    b1.start()

    for k in range(1, YS):
        v_copy(k).wait_recv()
    for j in range(YS):
        wf[:, j * width:(j + 1) * width] = wfb[j]

    a1.wait_recv()
    b1.wait_recv()

    def add_into(at, got, got_at, size):
        dw[rows(at, size), :] += got[rows(got_at, size), :]

    add_into(give_a2, ra1, (1 - bit2) * q2, q2)
    add_into(give_b2, rb1, (1 - bit1) * q2, q2)
    a2.start()
    b2.start()
    add_into(fa, ra1, bit2 * q2, q2)
    add_into(fb, rb1, bit1 * q2, q2)

    for i in range(2):
        arrive(p_copies(order(i)))
        start(p_relays(order(i)))

    a2.wait_recv()
    b2.wait_recv()
    ze[0:q2, :] = dw[rows(fa, q2), :] + ra2[...]
    ze[q2:2 * q2, :] = dw[rows(fb, q2), :] + rb2[...]

    def loop_z(f):
        def body(k, _):
            f(k)
            return 0

        lax.fori_loop(1, nz, body, 0)

    loop_z(lambda k: z_copy(k).start())

    for i in range(2, BUNDLES):
        arrive(p_copies(order(i)))
        start(p_relays(order(i)))

    def gx_copy(b):
        return pltpu.make_async_copy(gxv.at[b], gx_hbm.at[:, cols(b)], o_sem.at[b])

    def rows_grad(i, _):
        b = order(i)
        arrive(p_relays(b))
        gxv[b] = dot(wf[...], gp[b], ((1,), (0,))).astype(BF16)
        gx_copy(b).start()
        return 0

    lax.fori_loop(0, BUNDLES, rows_grad, 0)

    loop_z(lambda k: z_copy(k).wait_recv())

    def add_z(k, total):
        return total + zr[k]

    total = lax.fori_loop(1, nz, add_z, ze[rows(zi * piece, piece), :])
    fin[rows(spot(zi), piece), :] = (total * norm).astype(BF16)
    loop_z(lambda k: f_copy(k).start())
    loop_z(lambda k: f_copy(k).wait_recv())
    ag_a2.start()
    ag_b2.start()
    ag_a2.wait_recv()
    ag_b2.wait_recv()
    ag_a1.start()
    ag_b1.start()
    ag_a1.wait_recv()
    ag_b1.wait_recv()
    ag_core.start()

    def fin_out(n):
        return pltpu.make_async_copy(
            fin.at[n * width:(n + 1) * width], fin_hbm.at[:, n * LANES:(n + 1) * LANES],
            o_sem.at[BUNDLES + n])

    ag_core.wait_recv()
    for n in range(d_model // LANES):
        fin_out(n).start()

    for b in range(BUNDLES):
        for cp in g_copy(b) + x_copies(b) + x_relays(b) + p_copies(b) + p_relays(b):
            cp.wait_send()
        gx_copy(b).wait()
    for k in range(1, YS):
        w_copy(k).wait_send()
        v_copy(k).wait_send()
    for cp in (core_rs, a1, b1, a2, b2, ag_a2, ag_b2, ag_a1, ag_b1, ag_core):
        cp.wait_send()
    loop_z(lambda k: z_copy(k).wait_send())
    loop_z(lambda k: f_copy(k).wait_send())
    for n in range(d_model // LANES):
        fin_out(n).wait()


def shards(patches, counts, qkv_weight, grad_context):
    n_dp = lax.axis_size("dp")
    nz = n_dp // (XS * CORES)
    feat, width, grads = patches.shape[1], qkv_weight.shape[1], grad_context.shape[1]
    d_model = YS * feat
    blocks = d_model // LANES
    parts = n_dp
    unit = -(-(blocks * width) // (parts * 16)) * 16
    flat = unit * parts
    wide = 2 * LANES * (-(-blocks // 2))
    half = flat // 2
    q1, q2 = half // 4, half // 8
    dma = pltpu.SemaphoreType.DMA
    any_spec = pl.BlockSpec(memory_space=pl.ANY)
    gx, fin = pl.pallas_call(
        functools.partial(kernel, n_dp),
        out_shape=(
            jax.ShapeDtypeStruct((feat, SEQ), BF16),
            jax.ShapeDtypeStruct((width, d_model), BF16),
        ),
        in_specs=[any_spec] * 3 + [pl.BlockSpec(memory_space=pltpu.SMEM)],
        out_specs=(any_spec, any_spec),
        scratch_shapes=[
            pltpu.VMEM((BUNDLES, wide, CAP), BF16),
            pltpu.VMEM((width, d_model), BF16),
            pltpu.VMEM((d_model, width), BF16),
            pltpu.VMEM((BUNDLES, TAG, CAP), BF16),
            pltpu.VMEM((BUNDLES, TAG, CAP), BF16),
            pltpu.VMEM((BUNDLES, grads, CAP), BF16),
            pltpu.VMEM((width, CAP), F32),
            pltpu.VMEM((grads, CAP), F32),
            pltpu.VMEM((width, CAP), F32),
            pltpu.VMEM((BUNDLES, YS * width, CAP), BF16),
            pltpu.VMEM((YS, feat, width), BF16),
            pltpu.VMEM((feat, YS * width), BF16),
            pltpu.VMEM((max(flat, wide // LANES * width), LANES), F32),
            pltpu.VMEM((half, LANES), F32),
            pltpu.VMEM((q1, LANES), F32),
            pltpu.VMEM((q2, LANES), F32),
            pltpu.VMEM((q1, LANES), F32),
            pltpu.VMEM((q2, LANES), F32),
            pltpu.VMEM((2 * q2, LANES), F32),
            pltpu.VMEM((nz, 2 * q2 // nz, LANES), F32),
            pltpu.VMEM((flat, LANES), BF16),
            pltpu.VMEM((BUNDLES, feat, CAP), BF16),
            dma((4, BUNDLES)), dma((4, BUNDLES)),
            dma((BUNDLES,)), dma((BUNDLES,)),
            dma((BUNDLES,)), dma((BUNDLES,)),
            dma((4, BUNDLES)), dma((4, BUNDLES)),
            dma((YS - 1,)), dma((YS - 1,)),
            dma((YS - 1,)), dma((YS - 1,)),
            dma((10,)), dma((10,)),
            dma((nz,)), dma((nz,)),
            dma((nz,)), dma((nz,)),
            dma((BUNDLES + 1,)), dma((BUNDLES + blocks,)),
        ],
        compiler_params=pltpu.CompilerParams(
            collective_id=0, has_side_effects=True, vmem_limit_bytes=60 * 1024 * 1024),
        name="layer",
    )(patches.T, grad_context.T, qkv_weight.T, counts[0])
    return gx.T, fin.T


def solution(mesh):
    in_specs = (P("dp", "mp"), P("dp", None, None), P(None, "mp"), P("dp", "mp"))
    out_specs = (P("dp", "mp"), P(None, "mp"))
    return jax.shard_map(shards, mesh=mesh, in_specs=in_specs, out_specs=out_specs, check_vma=False)
```

```python
import functools
import math

import jax
import jax.numpy as jnp
from jax import lax
from jax.experimental import pallas as pl
from jax.experimental.pallas import tpu as pltpu
from jax.sharding import PartitionSpec as P

HD = 88
IMGS = 4
BUNDLES = 4
CAP = 256
SEQ = 1024
YS = 4
XS = 4
CORES = 2
LANES = 128
SETS = 3
TAG = 16

F32 = jnp.float32
BF16 = jnp.bfloat16


def dot(a, b, dims):
    return lax.dot_general(a, b, (dims, ((), ())), preferred_element_type=F32)


def kernel(
    n_dp,
    x_hbm, g_hbm, w_hbm, counts,
    gx_hbm, fin_hbm,
    xt, wt, wn, tag, gt, gb, pk, up_all, gps, gp, wfb, wf, dw, c0, ra1, ra2, rb1, rb2, ze, zr, fin, gxv,
    x_ss, x_rs, g_ss, g_rs, t_ss, t_rs, p_ss, p_rs, w_ss, w_rs, v_ss, v_rs, d_ss, d_rs, z_ss, z_rs, f_ss, f_rs, l_sem, o_sem,
):
    feat = x_hbm.shape[0]
    width = w_hbm.shape[0]
    heads = width // (3 * HD)
    d_model = YS * feat
    nz = n_dp // (XS * CORES)
    stride = n_dp // BUNDLES
    scale = 1.0 / math.sqrt(HD)
    norm = 1.0 / math.sqrt(n_dp)
    part = fin.shape[0] // SETS
    half = part // CORES
    sub = half // 2
    q1 = sub // 2
    q2 = q1 // 2
    piece = 2 * q2 // nz

    dp = lax.axis_index("dp")
    me = lax.axis_index("mp")
    right, left, far = (me + 1) % YS, (me + 3) % YS, (me + 2) % YS
    core = dp % CORES
    xi = (dp // CORES) % XS
    zi = dp // (XS * CORES)
    base_xz = zi * (XS * CORES)
    mate = {"dp": dp + 1 - 2 * core}
    even = xi % 2
    near1 = {"dp": base_xz + (xi + 1 - 2 * even) * CORES + core}
    near2 = {"dp": base_xz + ((xi + 3 - 2 * even) % XS) * CORES + core}
    bit1 = ((xi + 1) // 2) % 2
    bit2 = xi // 2

    def z_peer(k):
        return {"dp": ((zi + k) % nz) * (XS * CORES) + xi * CORES + core}

    def remote(src, dst, ss, rs, dev):
        return pltpu.make_async_remote_copy(
            src_ref=src, dst_ref=dst, send_sem=ss, recv_sem=rs,
            device_id=dev, device_id_type=pl.DeviceIdType.MESH,
        )

    def rows(start, size):
        return pl.ds(pl.multiple_of(start, 16), size)

    def order(i):
        return (3 * i) % BUNDLES

    def cols(b):
        return pl.ds(pl.multiple_of(b * CAP, CAP), CAP)

    def g_copy(b):
        off = stride // 2 + b * stride
        to = {"dp": (dp + off) % n_dp}
        return (
            remote(tag.at[b], gt.at[b], t_ss.at[b], t_rs.at[b], to),
            remote(g_hbm.at[:, cols(b)], gb.at[b], g_ss.at[b], g_rs.at[b], to),
        )

    def x_copies(b):
        src = x_hbm.at[:, cols(b)]
        r = rows(me * feat, feat)
        return (
            remote(src, xt.at[b, r], x_ss.at[0, b], x_rs.at[0, b], {"mp": right}),
            remote(src, xt.at[b, r], x_ss.at[1, b], x_rs.at[1, b], {"mp": left}),
        )

    def x_relays(b):
        r = rows(left * feat, feat // 2)
        s = rows(right * feat + feat // 2, feat // 2)
        return (
            remote(xt.at[b, r], xt.at[b, r], x_ss.at[2, b], x_rs.at[2, b], {"mp": right}),
            remote(xt.at[b, s], xt.at[b, s], x_ss.at[3, b], x_rs.at[3, b], {"mp": left}),
        )

    def x_local(b):
        return pltpu.make_async_copy(
            x_hbm.at[:, cols(b)], xt.at[b, rows(me * feat, feat)], l_sem.at[b])

    def p_copies(b):
        r = rows(me * width, width)
        return (
            remote(gp.at[b, r], gp.at[b, r], p_ss.at[0, b], p_rs.at[0, b], {"mp": right}),
            remote(gp.at[b, r], gp.at[b, r], p_ss.at[1, b], p_rs.at[1, b], {"mp": left}),
        )

    def p_relays(b):
        r = rows(left * width, 256)
        s = rows(right * width + 256, width - 256)
        return (
            remote(gp.at[b, r], gp.at[b, r], p_ss.at[2, b], p_rs.at[2, b], {"mp": right}),
            remote(gp.at[b, s], gp.at[b, s], p_ss.at[3, b], p_rs.at[3, b], {"mp": left}),
        )

    fh = feat // CORES

    def w_copy(k):
        to = (me + k) % YS
        return remote(
            wn.at[rows(to * feat + core * fh, fh)], wfb.at[me, rows(core * fh, fh)],
            w_ss.at[k - 1], w_rs.at[k - 1], {"mp": to},
        )

    def v_copy(k):
        who = (me + YS - k) % YS
        r = rows(core * fh, fh)
        return remote(wfb.at[who, r], wfb.at[who, r], v_ss.at[k - 1], v_rs.at[k - 1], mate)

    def spans(s):
        oa = s * part + core * half
        ob = oa + sub
        keep_a, keep_b = oa + bit1 * q1, ob + bit2 * q1
        return oa, ob, keep_a, keep_b, keep_a + bit2 * q2, keep_b + bit1 * q2

    def core_sum(s):
        r = rows(s * part + (1 - core) * half, half)
        return remote(dw.at[r], c0.at[s], d_ss.at[s, 0], d_rs.at[s, 0], mate)

    def x_sum1(s):
        oa, ob = spans(s)[:2]
        ra, rb = rows(oa + (1 - bit1) * q1, q1), rows(ob + (1 - bit2) * q1, q1)
        return (
            remote(dw.at[ra], ra1.at[s], d_ss.at[s, 1], d_rs.at[s, 1], near1),
            remote(dw.at[rb], rb1.at[s], d_ss.at[s, 2], d_rs.at[s, 2], near2),
        )

    def gives(s):
        keep_a, keep_b = spans(s)[2:4]
        return keep_a + (1 - bit2) * q2, keep_b + (1 - bit1) * q2

    def x_sum2(s):
        ga, gb_ = gives(s)
        return (
            remote(dw.at[rows(ga, q2)], ra2.at[s], d_ss.at[s, 3], d_rs.at[s, 3], near2),
            remote(dw.at[rows(gb_, q2)], rb2.at[s], d_ss.at[s, 4], d_rs.at[s, 4], near1),
        )

    def z_copy(s, k):
        to = (zi + k) % nz
        return remote(ze.at[s, rows(to * piece, piece)], zr.at[s, k], z_ss.at[s, k], z_rs.at[s, k], z_peer(k))

    def spot(s):
        fa, fb = spans(s)[4:]
        return jnp.where(zi < nz // 2, fa + zi * piece, fb + (zi - nz // 2) * piece)

    def f_copy(s, k):
        r = rows(spot(s), piece)
        return remote(fin.at[r], fin.at[r], f_ss.at[s, k], f_rs.at[s, k], z_peer(k))

    def same(s, start, size, i, dev):
        r = rows(start, size)
        return remote(fin.at[r], fin.at[r], d_ss.at[s, i], d_rs.at[s, i], dev)

    def x_gather2(s):
        fa, fb = spans(s)[4:]
        return same(s, fa, q2, 5, near2), same(s, fb, q2, 6, near1)

    def x_gather1(s):
        keep_a, keep_b = spans(s)[2:4]
        return same(s, keep_a, q1, 7, near1), same(s, keep_b, q1, 8, near2)

    def core_gather(s):
        return (same(s, s * part + core * half, half, 9, mate),)

    barrier = pltpu.get_barrier_semaphore()
    mesh_id = pl.DeviceIdType.MESH

    def greet(k, _):
        pl.semaphore_signal(barrier, inc=1, device_id=z_peer(k), device_id_type=mesh_id)
        return 0

    lax.fori_loop(1, nz, greet, 0)
    for dev in [{"mp": right}, {"mp": left}, {"mp": far}, mate, near1, near2]:
        pl.semaphore_signal(barrier, inc=1, device_id=dev, device_id_type=mesh_id)
    w_local = pltpu.make_async_copy(w_hbm, wt, l_sem.at[BUNDLES])
    w_local.start()
    for i in range(BUNDLES):
        x_local(order(i)).start()

    slot = lax.broadcasted_iota(jnp.int32, (TAG, CAP), 1)
    for b in range(BUNDLES):
        end = counts[b, 0]
        ids = jnp.where(slot >= end, 1, 0)
        for i in range(1, IMGS):
            end = end + counts[b, i]
            ids = ids + jnp.where(slot >= end, 1, 0)
        tag[b] = jnp.where(slot < end, ids - IMGS, slot).astype(F32).astype(BF16)
    for b in range(BUNDLES):
        xt[b, d_model:, :] = jnp.zeros((xt.shape[1] - d_model, CAP), BF16)
    pl.semaphore_wait(barrier, 6 + nz - 1)

    def start(copies):
        for cp in copies:
            cp.start()

    def arrive(copies):
        for cp in copies:
            cp.wait_recv()

    start(x_copies(0))
    for i in range(BUNDLES):
        start(g_copy(order(i)))
    start(x_copies(order(1)))
    w_local.wait()
    for n in range(d_model // LANES):
        wn[n * LANES:(n + 1) * LANES, :] = wt[:, n * LANES:(n + 1) * LANES].T
    for i in range(BUNDLES):
        x_local(order(i)).wait()
    wfb[me] = wn[rows(me * feat, feat), :]

    arrive(x_copies(0))
    start(x_relays(0))
    start(x_copies(order(2)))

    def bundle(i, _):
        b = order(i)

        @pl.when(i < BUNDLES - 1)
        def _():
            nxt = order(i + 1)
            arrive(x_copies(nxt))
            start(x_relays(nxt))

        @pl.when(i == 0)
        def _():
            start(x_copies(order(3)))

        @pl.when(i == 2)
        def _():
            for k in range(1, YS):
                w_copy(k).start()
            start(p_copies(order(0)))
            start(p_copies(order(1)))

        @pl.when(i == 3)
        def _():
            start(p_copies(order(2)))

        arrive(x_relays(b))
        pk[...] = dot(wt[...], xt[b, 0:d_model, :], ((1,), (0,)))
        arrive(g_copy(b))
        tags = gt[b].astype(F32)[0:8]
        allowed = tags[0:1, :] == tags.T[:, 0:1]
        up_all[...] = jnp.where(tags[0:1, :] < 0, gb[b].astype(F32), 0.0)
        for h in range(heads):
            o = h * 3 * HD
            query = pk[o:o + HD, :].astype(BF16)
            key = pk[o + HD:o + 2 * HD, :].astype(BF16)
            value = pk[o + 2 * HD:o + 3 * HD, :].astype(BF16)
            up = up_all[h * HD:(h + 1) * HD, :].astype(BF16)
            scores = dot(query, key, ((0,), (0,))) * scale
            masked = jnp.where(allowed, scores, -1e30)
            top = jnp.max(masked, axis=1, keepdims=True)
            exponent = jnp.where(allowed, jnp.exp(masked - top), 0.0)
            probs = exponent * (1.0 / jnp.sum(exponent, axis=1, keepdims=True))
            grad_probs = dot(up, value, ((0,), (0,)))
            row_dot = jnp.sum(probs * grad_probs, axis=1, keepdims=True)
            logits = (probs * (grad_probs - row_dot) * scale).astype(BF16)
            gps[o:o + HD, :] = dot(key, logits, ((1,), (1,)))
            gps[o + HD:o + 2 * HD, :] = dot(query, logits, ((1,), (0,)))
            gps[o + 2 * HD:o + 3 * HD, :] = dot(up, probs.astype(BF16), ((1,), (0,)))
        gp[b, rows(me * width, width), :] = gps[...].astype(BF16)
        return 0

    lax.fori_loop(0, BUNDLES, bundle, 0)
    start(p_copies(order(3)))

    mine = rows(me * width, width)

    def weight_block(n, _):
        block = rows(n * 2 * LANES, 2 * LANES)
        total = dot(gp[0, mine, :], xt[0, block, :], ((1,), (1,)))
        for b in range(1, BUNDLES):
            total += dot(gp[b, mine, :], xt[b, block, :], ((1,), (1,)))
        at = n * 2 * width
        dw[rows(at, width), :] = total[:, :LANES]
        dw[rows(at + width, width), :] = total[:, LANES:]
        return 0

    n_blocks = xt.shape[1] // (2 * LANES)
    for s in range(SETS):
        lax.fori_loop(s * n_blocks // SETS, (s + 1) * n_blocks // SETS, weight_block, 0)
        core_sum(s).start()

    def add_into(at, got, got_at, size):
        dw[rows(at, size), :] += got[rows(got_at, size), :]

    def add_core(s):
        core_sum(s).wait_recv()
        add_into(s * part + core * half, c0.at[s], 0, half)

    def add_x1(s):
        arrive(x_sum1(s))
        ga, gb_ = gives(s)
        fa, fb = spans(s)[4:]
        add_into(ga, ra1.at[s], (1 - bit2) * q2, q2)
        add_into(gb_, rb1.at[s], (1 - bit1) * q2, q2)
        start(x_sum2(s))
        add_into(fa, ra1.at[s], bit2 * q2, q2)
        add_into(fb, rb1.at[s], bit1 * q2, q2)

    def loop_z(f):
        def body(k, _):
            f(k)
            return 0

        lax.fori_loop(1, nz, body, 0)

    def add_x2(s):
        arrive(x_sum2(s))
        fa, fb = spans(s)[4:]
        ze[s, 0:q2, :] = dw[rows(fa, q2), :] + ra2[s]
        ze[s, q2:2 * q2, :] = dw[rows(fb, q2), :] + rb2[s]
        loop_z(lambda k: z_copy(s, k).start())

    def add_z(s):
        loop_z(lambda k: z_copy(s, k).wait_recv())
        total = ze[s, rows(zi * piece, piece), :]
        for k in range(1, nz):
            total += zr[s, k]
        fin[rows(spot(s), piece), :] = (total * norm).astype(BF16)
        loop_z(lambda k: f_copy(s, k).start())

    def pass_on(i):
        arrive(p_copies(order(i)))
        start(p_relays(order(i)))

    def gx_copy(b):
        return pltpu.make_async_copy(gxv.at[b], gx_hbm.at[:, cols(b)], o_sem.at[b])

    def rows_grad(i):
        b = order(i)
        arrive(p_relays(b))
        gxv[b] = dot(wf[...], gp[b], ((1,), (0,))).astype(BF16)
        gx_copy(b).start()

    def gathered_z(s):
        loop_z(lambda k: f_copy(s, k).wait_recv())
        start(x_gather2(s))

    def gathered_x2(s):
        arrive(x_gather2(s))
        start(x_gather1(s))

    def gathered_x1(s):
        arrive(x_gather1(s))
        start(core_gather(s))

    def fin_out(n):
        return pltpu.make_async_copy(
            fin.at[n * width:(n + 1) * width], fin_hbm.at[:, n * LANES:(n + 1) * LANES],
            o_sem.at[BUNDLES + n])

    def whole_blocks(s):
        return min(d_model // LANES, s * part // width)

    def gathered_core(s):
        arrive(core_gather(s))
        for n in range(whole_blocks(s), whole_blocks(s + 1)):
            fin_out(n).start()

    add_core(0)
    start(x_sum1(0))
    add_core(1)
    start(x_sum1(1))
    add_core(2)
    add_x1(0)
    start(x_sum1(2))
    add_x1(1)
    add_x2(0)
    add_x1(2)
    add_x2(1)
    for k in range(1, YS):
        w_copy(k).wait_recv()
        v_copy(k).start()
    add_x2(2)
    pass_on(0)
    pass_on(1)
    for k in range(1, YS):
        v_copy(k).wait_recv()
    for j in range(YS):
        wf[:, j * width:(j + 1) * width] = wfb[j]
    add_z(0)
    pass_on(2)
    add_z(1)
    pass_on(3)
    add_z(2)
    gathered_z(0)
    rows_grad(0)
    gathered_z(1)
    gathered_x2(0)
    rows_grad(1)
    gathered_x1(0)
    gathered_x2(1)
    rows_grad(2)
    gathered_z(2)
    gathered_x1(1)
    gathered_core(0)
    rows_grad(3)
    gathered_x2(2)
    gathered_core(1)
    gathered_x1(2)
    gathered_core(2)

    for b in range(BUNDLES):
        for cp in g_copy(b) + x_copies(b) + x_relays(b) + p_copies(b) + p_relays(b):
            cp.wait_send()
        gx_copy(b).wait()
    for k in range(1, YS):
        w_copy(k).wait_send()
        v_copy(k).wait_send()
    for s in range(SETS):
        for cp in x_sum1(s) + x_sum2(s) + x_gather2(s) + x_gather1(s) + core_gather(s):
            cp.wait_send()
        core_sum(s).wait_send()
        loop_z(lambda k: z_copy(s, k).wait_send())
        loop_z(lambda k: f_copy(s, k).wait_send())
    for n in range(d_model // LANES):
        fin_out(n).wait()


def shards(patches, counts, qkv_weight, grad_context):
    n_dp = lax.axis_size("dp")
    nz = n_dp // (XS * CORES)
    feat, width, grads = patches.shape[1], qkv_weight.shape[1], grad_context.shape[1]
    d_model = YS * feat
    blocks = d_model // LANES
    parts = n_dp
    unit = -(-(blocks * width) // (parts * SETS * 16)) * SETS * 16
    flat = unit * parts
    wide = 2 * LANES * (-(-blocks // 2))
    half = flat // SETS // CORES
    q1, q2 = half // 4, half // 8
    dma = pltpu.SemaphoreType.DMA
    any_spec = pl.BlockSpec(memory_space=pl.ANY)
    gx, fin = pl.pallas_call(
        functools.partial(kernel, n_dp),
        out_shape=(
            jax.ShapeDtypeStruct((feat, SEQ), BF16),
            jax.ShapeDtypeStruct((width, d_model), BF16),
        ),
        in_specs=[any_spec] * 3 + [pl.BlockSpec(memory_space=pltpu.SMEM)],
        out_specs=(any_spec, any_spec),
        scratch_shapes=[
            pltpu.VMEM((BUNDLES, wide, CAP), BF16),
            pltpu.VMEM((width, d_model), BF16),
            pltpu.VMEM((d_model, width), BF16),
            pltpu.VMEM((BUNDLES, TAG, CAP), BF16),
            pltpu.VMEM((BUNDLES, TAG, CAP), BF16),
            pltpu.VMEM((BUNDLES, grads, CAP), BF16),
            pltpu.VMEM((width, CAP), F32),
            pltpu.VMEM((grads, CAP), F32),
            pltpu.VMEM((width, CAP), F32),
            pltpu.VMEM((BUNDLES, YS * width, CAP), BF16),
            pltpu.VMEM((YS, feat, width), BF16),
            pltpu.VMEM((feat, YS * width), BF16),
            pltpu.VMEM((max(flat, wide // LANES * width), LANES), F32),
            pltpu.VMEM((SETS, half, LANES), F32),
            pltpu.VMEM((SETS, q1, LANES), F32),
            pltpu.VMEM((SETS, q2, LANES), F32),
            pltpu.VMEM((SETS, q1, LANES), F32),
            pltpu.VMEM((SETS, q2, LANES), F32),
            pltpu.VMEM((SETS, 2 * q2, LANES), F32),
            pltpu.VMEM((SETS, nz, 2 * q2 // nz, LANES), F32),
            pltpu.VMEM((flat, LANES), BF16),
            pltpu.VMEM((BUNDLES, feat, CAP), BF16),
            dma((4, BUNDLES)), dma((4, BUNDLES)),
            dma((BUNDLES,)), dma((BUNDLES,)),
            dma((BUNDLES,)), dma((BUNDLES,)),
            dma((4, BUNDLES)), dma((4, BUNDLES)),
            dma((YS - 1,)), dma((YS - 1,)),
            dma((YS - 1,)), dma((YS - 1,)),
            dma((SETS, 10)), dma((SETS, 10)),
            dma((SETS, nz)), dma((SETS, nz)),
            dma((SETS, nz)), dma((SETS, nz)),
            dma((BUNDLES + 1,)), dma((BUNDLES + blocks,)),
        ],
        compiler_params=pltpu.CompilerParams(
            collective_id=0, has_side_effects=True, vmem_limit_bytes=60 * 1024 * 1024),
        name="layer",
    )(patches.T, grad_context.T, qkv_weight.T, counts[0])
    return gx.T, fin.T


def solution(mesh):
    in_specs = (P("dp", "mp"), P("dp", None, None), P(None, "mp"), P("dp", "mp"))
    out_specs = (P("dp", "mp"), P(None, "mp"))
    return jax.shard_map(shards, mesh=mesh, in_specs=in_specs, out_specs=out_specs, check_vma=False)
```

```python
import functools
import math

import jax
import jax.numpy as jnp
from jax import lax
from jax.experimental import pallas as pl
from jax.experimental.pallas import tpu as pltpu
from jax.sharding import PartitionSpec as P

HD = 88
IMGS = 4
BUNDLES = 4
CAP = 256
SEQ = 1024
YS = 4
XS = 4
CORES = 2
LANES = 128
SETS = 3
TAG = 16

F32 = jnp.float32
BF16 = jnp.bfloat16


def dot(a, b, dims):
    return lax.dot_general(a, b, (dims, ((), ())), preferred_element_type=F32)


def kernel(
    n_dp,
    x_hbm, g_hbm, w_hbm, counts,
    gx_out, fin_out,
    xt, wt, wn, tag, gt, gb, pk, up_all, gps, gp, wfb, wf, dw, c0, ra1, ra2, rb1, rb2, ze, rz, zh, zr, fin,
    x_ss, x_rs, g_ss, g_rs, t_ss, t_rs, p_ss, p_rs, w_ss, w_rs, v_ss, v_rs, d_ss, d_rs, z_ss, z_rs, f_ss, f_rs, l_sem,
):
    feat = x_hbm.shape[0]
    width = w_hbm.shape[0]
    heads = width // (3 * HD)
    d_model = YS * feat
    nz = n_dp // (XS * CORES)
    stride = n_dp // BUNDLES
    scale = 1.0 / math.sqrt(HD)
    norm = 1.0 / math.sqrt(n_dp)
    part = fin.shape[0] // SETS
    half = part // CORES
    sub = half // 2
    q1 = sub // 2
    q2 = q1 // 2
    q3 = q2 // 2
    piece = 2 * q2 // nz

    dp = lax.axis_index("dp")
    me = lax.axis_index("mp")
    right, left, far = (me + 1) % YS, (me + 3) % YS, (me + 2) % YS
    core = dp % CORES
    xi = (dp // CORES) % XS
    zi = dp // (XS * CORES)
    base_xz = zi * (XS * CORES)
    mate = {"dp": dp + 1 - 2 * core}
    even = xi % 2
    near1 = {"dp": base_xz + (xi + 1 - 2 * even) * CORES + core}
    near2 = {"dp": base_xz + ((xi + 3 - 2 * even) % XS) * CORES + core}
    bit1 = ((xi + 1) // 2) % 2
    bit2 = xi // 2

    par, zg = zi % 2, zi // 2
    zn1 = {"dp": dp + (1 - 2 * par) * (XS * CORES)}
    zn2 = {"dp": (dp + n_dp + (2 * par - 1) * (XS * CORES)) % n_dp}

    def z_peer(k):
        return {"dp": ((zi + k) % nz) * (XS * CORES) + xi * CORES + core}

    def remote(src, dst, ss, rs, dev):
        return pltpu.make_async_remote_copy(
            src_ref=src, dst_ref=dst, send_sem=ss, recv_sem=rs,
            device_id=dev, device_id_type=pl.DeviceIdType.MESH,
        )

    def rows(start, size):
        return pl.ds(pl.multiple_of(start, 16), size)

    def order(i):
        return (3 * i) % BUNDLES

    def cols(b):
        return pl.ds(pl.multiple_of(b * CAP, CAP), CAP)

    def g_copy(b):
        off = stride // 2 + b * stride
        to = {"dp": (dp + off) % n_dp}
        return (
            remote(tag.at[b], gt.at[b], t_ss.at[b], t_rs.at[b], to),
            remote(g_hbm.at[:, cols(b)], gb.at[b], g_ss.at[b], g_rs.at[b], to),
        )

    def x_copies(b):
        src = x_hbm.at[:, cols(b)]
        r = rows(me * feat, feat)
        return (
            remote(src, xt.at[b, r], x_ss.at[0, b], x_rs.at[0, b], {"mp": right}),
            remote(src, xt.at[b, r], x_ss.at[1, b], x_rs.at[1, b], {"mp": left}),
        )

    def x_relays(b):
        r = rows(left * feat, feat // 2)
        s = rows(right * feat + feat // 2, feat // 2)
        return (
            remote(xt.at[b, r], xt.at[b, r], x_ss.at[2, b], x_rs.at[2, b], {"mp": right}),
            remote(xt.at[b, s], xt.at[b, s], x_ss.at[3, b], x_rs.at[3, b], {"mp": left}),
        )

    def x_local(b):
        return pltpu.make_async_copy(
            x_hbm.at[:, cols(b)], xt.at[b, rows(me * feat, feat)], l_sem.at[b])

    def p_copies(b):
        r = rows(me * width, width)
        return (
            remote(gp.at[b, r], gp.at[b, r], p_ss.at[0, b], p_rs.at[0, b], {"mp": right}),
            remote(gp.at[b, r], gp.at[b, r], p_ss.at[1, b], p_rs.at[1, b], {"mp": left}),
        )

    def p_relays(b):
        r = rows(left * width, 256)
        s = rows(right * width + 256, width - 256)
        return (
            remote(gp.at[b, r], gp.at[b, r], p_ss.at[2, b], p_rs.at[2, b], {"mp": right}),
            remote(gp.at[b, s], gp.at[b, s], p_ss.at[3, b], p_rs.at[3, b], {"mp": left}),
        )

    fh = feat // CORES

    def w_copy(k):
        to = (me + k) % YS
        return remote(
            wn.at[rows(to * feat + core * fh, fh)], wfb.at[me, rows(core * fh, fh)],
            w_ss.at[k - 1], w_rs.at[k - 1], {"mp": to},
        )

    def v_copy(k):
        who = (me + YS - k) % YS
        r = rows(core * fh, fh)
        return remote(wfb.at[who, r], wfb.at[who, r], v_ss.at[k - 1], v_rs.at[k - 1], mate)

    def spans(s):
        oa = s * part + core * half
        ob = oa + sub
        keep_a, keep_b = oa + bit1 * q1, ob + bit2 * q1
        return oa, ob, keep_a, keep_b, keep_a + bit2 * q2, keep_b + bit1 * q2

    def core_sum(s):
        r = rows(s * part + (1 - core) * half, half)
        return remote(dw.at[r], c0.at[s], d_ss.at[s, 0], d_rs.at[s, 0], mate)

    def x_sum1(s):
        oa, ob = spans(s)[:2]
        ra, rb = rows(oa + (1 - bit1) * q1, q1), rows(ob + (1 - bit2) * q1, q1)
        return (
            remote(dw.at[ra], ra1.at[s], d_ss.at[s, 1], d_rs.at[s, 1], near1),
            remote(dw.at[rb], rb1.at[s], d_ss.at[s, 2], d_rs.at[s, 2], near2),
        )

    def gives(s):
        keep_a, keep_b = spans(s)[2:4]
        return keep_a + (1 - bit2) * q2, keep_b + (1 - bit1) * q2

    def x_sum2(s):
        ga, gb_ = gives(s)
        return (
            remote(dw.at[rows(ga, q2)], ra2.at[s], d_ss.at[s, 3], d_rs.at[s, 3], near2),
            remote(dw.at[rows(gb_, q2)], rb2.at[s], d_ss.at[s, 4], d_rs.at[s, 4], near1),
        )

    def z_half(s):
        give = (1 - par) * q3
        return (
            remote(ze.at[s, rows(give, q3)], rz.at[s, 0:q3], d_ss.at[s, 10], d_rs.at[s, 10], zn1),
            remote(ze.at[s, rows(q2 + give, q3)], rz.at[s, q3:2 * q3], d_ss.at[s, 11], d_rs.at[s, 11], zn2),
        )

    def z_copy(s, k):
        to = ((zi + 2 * k) % nz) // 2
        return remote(zh.at[s, rows(to * piece, piece)], zr.at[s, k], z_ss.at[s, k], z_rs.at[s, k], z_peer(2 * k))

    def spot(s):
        fa, fb = spans(s)[4:]
        at = par * q3 + zg * piece
        return jnp.where(zg < nz // 4, fa + at, fb + at - q3)

    def f_copy(s, k):
        r = rows(spot(s), piece)
        return remote(fin.at[r], fin.at[r], f_ss.at[s, k], f_rs.at[s, k], z_peer(k))

    def same(s, start, size, i, dev):
        r = rows(start, size)
        return remote(fin.at[r], fin.at[r], d_ss.at[s, i], d_rs.at[s, i], dev)

    def x_gather2(s):
        fa, fb = spans(s)[4:]
        return same(s, fa, q2, 5, near2), same(s, fb, q2, 6, near1)

    def x_gather1(s):
        keep_a, keep_b = spans(s)[2:4]
        return same(s, keep_a, q1, 7, near1), same(s, keep_b, q1, 8, near2)

    def core_gather(s):
        return (same(s, s * part + core * half, half, 9, mate),)

    barrier = pltpu.get_barrier_semaphore()
    mesh_id = pl.DeviceIdType.MESH

    def greet(k, _):
        pl.semaphore_signal(barrier, inc=1, device_id=z_peer(k), device_id_type=mesh_id)
        return 0

    lax.fori_loop(1, nz, greet, 0)
    for dev in [{"mp": right}, {"mp": left}, {"mp": far}, mate, near1, near2]:
        pl.semaphore_signal(barrier, inc=1, device_id=dev, device_id_type=mesh_id)
    w_local = pltpu.make_async_copy(w_hbm, wt, l_sem.at[BUNDLES])
    w_local.start()
    for i in range(BUNDLES):
        x_local(order(i)).start()

    slot = lax.broadcasted_iota(jnp.int32, (TAG, CAP), 1)
    for b in range(BUNDLES):
        end = counts[b, 0]
        ids = jnp.where(slot >= end, 1, 0)
        for i in range(1, IMGS):
            end = end + counts[b, i]
            ids = ids + jnp.where(slot >= end, 1, 0)
        tag[b] = jnp.where(slot < end, ids - IMGS, slot).astype(F32).astype(BF16)
    for b in range(BUNDLES):
        xt[b, d_model:, :] = jnp.zeros((xt.shape[1] - d_model, CAP), BF16)
    pl.semaphore_wait(barrier, 6 + nz - 1)

    def start(copies):
        for cp in copies:
            cp.start()

    def arrive(copies):
        for cp in copies:
            cp.wait_recv()

    start(x_copies(0))
    for i in range(BUNDLES):
        start(g_copy(order(i)))
    start(x_copies(order(1)))
    w_local.wait()
    for n in range(d_model // LANES):
        wn[n * LANES:(n + 1) * LANES, :] = wt[:, n * LANES:(n + 1) * LANES].T
    for i in range(BUNDLES):
        x_local(order(i)).wait()
    wfb[me] = wn[rows(me * feat, feat), :]

    arrive(x_copies(0))
    start(x_relays(0))
    start(x_copies(order(2)))

    def bundle(i, _):
        b = order(i)

        @pl.when(i < BUNDLES - 1)
        def _():
            nxt = order(i + 1)
            arrive(x_copies(nxt))
            start(x_relays(nxt))

        @pl.when(i == 0)
        def _():
            start(x_copies(order(3)))

        @pl.when(i == 2)
        def _():
            for k in range(1, YS):
                w_copy(k).start()
            start(p_copies(order(0)))
            start(p_copies(order(1)))

        @pl.when(i == 3)
        def _():
            start(p_copies(order(2)))

        arrive(x_relays(b))
        pk[...] = dot(wt[...], xt[b, 0:d_model, :], ((1,), (0,)))
        arrive(g_copy(b))
        tags = gt[b].astype(F32)[0:8]
        allowed = tags[0:1, :] == tags.T[:, 0:1]
        up_all[...] = jnp.where(tags[0:1, :] < 0, gb[b].astype(F32), 0.0)
        for h in range(heads):
            o = h * 3 * HD
            query = pk[o:o + HD, :].astype(BF16)
            key = pk[o + HD:o + 2 * HD, :].astype(BF16)
            value = pk[o + 2 * HD:o + 3 * HD, :].astype(BF16)
            up = up_all[h * HD:(h + 1) * HD, :].astype(BF16)
            scores = dot(query, key, ((0,), (0,))) * scale
            masked = jnp.where(allowed, scores, -1e30)
            top = jnp.max(masked, axis=1, keepdims=True)
            exponent = jnp.where(allowed, jnp.exp(masked - top), 0.0)
            probs = exponent * (1.0 / jnp.sum(exponent, axis=1, keepdims=True))
            grad_probs = dot(up, value, ((0,), (0,)))
            row_dot = jnp.sum(probs * grad_probs, axis=1, keepdims=True)
            logits = (probs * (grad_probs - row_dot) * scale).astype(BF16)
            gps[o:o + HD, :] = dot(key, logits, ((1,), (1,)))
            gps[o + HD:o + 2 * HD, :] = dot(query, logits, ((1,), (0,)))
            gps[o + 2 * HD:o + 3 * HD, :] = dot(up, probs.astype(BF16), ((1,), (0,)))
        gp[b, rows(me * width, width), :] = gps[...].astype(BF16)
        return 0

    lax.fori_loop(0, BUNDLES, bundle, 0)
    start(p_copies(order(3)))

    mine = rows(me * width, width)

    def weight_block(n, _):
        block = rows(n * 2 * LANES, 2 * LANES)
        total = dot(gp[0, mine, :], xt[0, block, :], ((1,), (1,)))
        for b in range(1, BUNDLES):
            total += dot(gp[b, mine, :], xt[b, block, :], ((1,), (1,)))
        at = n * 2 * width
        dw[rows(at, width), :] = total[:, :LANES]
        dw[rows(at + width, width), :] = total[:, LANES:]
        return 0

    n_blocks = xt.shape[1] // (2 * LANES)
    for s in range(SETS):
        lax.fori_loop(s * n_blocks // SETS, (s + 1) * n_blocks // SETS, weight_block, 0)
        core_sum(s).start()

    def add_into(at, got, got_at, size):
        dw[rows(at, size), :] += got[rows(got_at, size), :]

    def add_core(s):
        core_sum(s).wait_recv()
        add_into(s * part + core * half, c0.at[s], 0, half)

    def add_x1(s):
        arrive(x_sum1(s))
        ga, gb_ = gives(s)
        fa, fb = spans(s)[4:]
        add_into(ga, ra1.at[s], (1 - bit2) * q2, q2)
        add_into(gb_, rb1.at[s], (1 - bit1) * q2, q2)
        start(x_sum2(s))
        add_into(fa, ra1.at[s], bit2 * q2, q2)
        add_into(fb, rb1.at[s], bit1 * q2, q2)

    def loop_z(f):
        def body(k, _):
            f(k)
            return 0

        lax.fori_loop(1, nz, body, 0)

    def add_x2(s):
        arrive(x_sum2(s))
        fa, fb = spans(s)[4:]
        ze[s, 0:q2, :] = dw[rows(fa, q2), :] + ra2[s]
        ze[s, q2:2 * q2, :] = dw[rows(fb, q2), :] + rb2[s]
        start(z_half(s))

    def loop_zz(f):
        def body(k, _):
            f(k)
            return 0

        lax.fori_loop(1, nz // 2, body, 0)

    def add_z1(s):
        arrive(z_half(s))
        zh[s, 0:q3, :] = ze[s, rows(par * q3, q3), :] + rz[s, 0:q3, :]
        zh[s, q3:2 * q3, :] = ze[s, rows(q2 + par * q3, q3), :] + rz[s, q3:2 * q3, :]
        loop_zz(lambda k: z_copy(s, k).start())

    def add_z(s):
        loop_zz(lambda k: z_copy(s, k).wait_recv())
        total = zh[s, rows(zg * piece, piece), :]
        for k in range(1, nz // 2):
            total += zr[s, k]
        fin[rows(spot(s), piece), :] = (total * norm).astype(BF16)
        loop_z(lambda k: f_copy(s, k).start())

    def pass_on(i):
        arrive(p_copies(order(i)))
        start(p_relays(order(i)))

    def rows_grad(i):
        b = order(i)
        arrive(p_relays(b))
        gx_out[:, b * CAP:(b + 1) * CAP] = dot(wf[...], gp[b], ((1,), (0,))).astype(BF16)

    def gathered_z(s):
        loop_z(lambda k: f_copy(s, k).wait_recv())
        start(x_gather2(s))

    def gathered_x2(s):
        arrive(x_gather2(s))
        start(x_gather1(s))

    def gathered_x1(s):
        arrive(x_gather1(s))
        start(core_gather(s))

    def whole_blocks(s):
        return min(d_model // LANES, s * part // width)

    def gathered_core(s):
        arrive(core_gather(s))
        for n in range(whole_blocks(s), whole_blocks(s + 1)):
            fin_out[:, n * LANES:(n + 1) * LANES] = fin[n * width:(n + 1) * width, :]

    add_core(0)
    start(x_sum1(0))
    add_core(1)
    start(x_sum1(1))
    add_core(2)
    add_x1(0)
    start(x_sum1(2))
    add_x1(1)
    add_x2(0)
    add_x1(2)
    add_z1(0)
    add_x2(1)
    for k in range(1, YS):
        w_copy(k).wait_recv()
        v_copy(k).start()
    add_x2(2)
    add_z1(1)
    add_z1(2)
    pass_on(0)
    pass_on(1)
    for k in range(1, YS):
        v_copy(k).wait_recv()
    for j in range(YS):
        wf[:, j * width:(j + 1) * width] = wfb[j]
    add_z(0)
    pass_on(2)
    add_z(1)
    pass_on(3)
    add_z(2)
    gathered_z(0)
    rows_grad(0)
    gathered_z(1)
    gathered_x2(0)
    rows_grad(1)
    gathered_x1(0)
    gathered_x2(1)
    rows_grad(2)
    gathered_z(2)
    gathered_x1(1)
    gathered_core(0)
    rows_grad(3)
    gathered_x2(2)
    gathered_core(1)
    gathered_x1(2)
    gathered_core(2)

    for b in range(BUNDLES):
        for cp in g_copy(b) + x_copies(b) + x_relays(b) + p_copies(b) + p_relays(b):
            cp.wait_send()
    for k in range(1, YS):
        w_copy(k).wait_send()
        v_copy(k).wait_send()
    for s in range(SETS):
        for cp in x_sum1(s) + x_sum2(s) + z_half(s) + x_gather2(s) + x_gather1(s) + core_gather(s):
            cp.wait_send()
        core_sum(s).wait_send()
        loop_zz(lambda k: z_copy(s, k).wait_send())
        loop_z(lambda k: f_copy(s, k).wait_send())


def shards(patches, counts, qkv_weight, grad_context):
    n_dp = lax.axis_size("dp")
    nz = n_dp // (XS * CORES)
    feat, width, grads = patches.shape[1], qkv_weight.shape[1], grad_context.shape[1]
    d_model = YS * feat
    blocks = d_model // LANES
    parts = n_dp
    unit = -(-(blocks * width) // (parts * SETS * 16)) * SETS * 16
    flat = unit * parts
    wide = 2 * LANES * (-(-blocks // 2))
    half = flat // SETS // CORES
    q1, q2 = half // 4, half // 8
    operands = patches.T, grad_context.T, qkv_weight.T, counts[0]
    dma = pltpu.SemaphoreType.DMA
    hbm_spec = pl.BlockSpec(memory_space=pltpu.HBM)
    gx, fin = pl.pallas_call(
        functools.partial(kernel, n_dp),
        out_shape=(
            jax.ShapeDtypeStruct((feat, SEQ), BF16),
            jax.ShapeDtypeStruct((width, d_model), BF16),
        ),
        in_specs=[hbm_spec] * 3 + [pl.BlockSpec(memory_space=pltpu.SMEM)],
        out_specs=(pl.BlockSpec(memory_space=pltpu.VMEM),) * 2,
        scratch_shapes=[
            pltpu.VMEM((BUNDLES, wide, CAP), BF16),
            pltpu.VMEM((width, d_model), BF16),
            pltpu.VMEM((d_model, width), BF16),
            pltpu.VMEM((BUNDLES, TAG, CAP), BF16),
            pltpu.VMEM((BUNDLES, TAG, CAP), BF16),
            pltpu.VMEM((BUNDLES, grads, CAP), BF16),
            pltpu.VMEM((width, CAP), F32),
            pltpu.VMEM((grads, CAP), F32),
            pltpu.VMEM((width, CAP), F32),
            pltpu.VMEM((BUNDLES, YS * width, CAP), BF16),
            pltpu.VMEM((YS, feat, width), BF16),
            pltpu.VMEM((feat, YS * width), BF16),
            pltpu.VMEM((max(flat, wide // LANES * width), LANES), F32),
            pltpu.VMEM((SETS, half, LANES), F32),
            pltpu.VMEM((SETS, q1, LANES), F32),
            pltpu.VMEM((SETS, q2, LANES), F32),
            pltpu.VMEM((SETS, q1, LANES), F32),
            pltpu.VMEM((SETS, q2, LANES), F32),
            pltpu.VMEM((SETS, 2 * q2, LANES), F32),
            pltpu.VMEM((SETS, q2, LANES), F32),
            pltpu.VMEM((SETS, q2, LANES), F32),
            pltpu.VMEM((SETS, nz // 2, 2 * q2 // nz, LANES), F32),
            pltpu.VMEM((flat, LANES), BF16),
            dma((4, BUNDLES)), dma((4, BUNDLES)),
            dma((BUNDLES,)), dma((BUNDLES,)),
            dma((BUNDLES,)), dma((BUNDLES,)),
            dma((4, BUNDLES)), dma((4, BUNDLES)),
            dma((YS - 1,)), dma((YS - 1,)),
            dma((YS - 1,)), dma((YS - 1,)),
            dma((SETS, 12)), dma((SETS, 12)),
            dma((SETS, nz // 2)), dma((SETS, nz // 2)),
            dma((SETS, nz)), dma((SETS, nz)),
            dma((BUNDLES + 1,)),
        ],
        compiler_params=pltpu.CompilerParams(
            collective_id=0, has_side_effects=True, vmem_limit_bytes=50 * 1024 * 1024),
        name="layer",
    )(*[pltpu.with_memory_space_constraint(a, pltpu.HBM) for a in operands])
    return gx.T, fin.T


def solution(mesh):
    in_specs = (P("dp", "mp"), P("dp", None, None), P(None, "mp"), P("dp", "mp"))
    out_specs = (P("dp", "mp"), P(None, "mp"))
    return jax.shard_map(shards, mesh=mesh, in_specs=in_specs, out_specs=out_specs, check_vma=False)
```

```python
import functools
import math

import jax
import jax.numpy as jnp
from jax import lax
from jax.experimental import pallas as pl
from jax.experimental.pallas import tpu as pltpu
from jax.sharding import PartitionSpec as P

HD = 88
IMGS = 4
BUNDLES = 4
CAP = 256
SEQ = 1024
YS = 4
XS = 4
CORES = 2
LANES = 128
SETS = 3
TAG = 16

F32 = jnp.float32
BF16 = jnp.bfloat16


def dot(a, b, dims):
    return lax.dot_general(a, b, (dims, ((), ())), preferred_element_type=F32)


def kernel(
    n_dp,
    x_hbm, g_hbm, w_hbm, counts,
    gx_out, fin_out,
    xt, wt, wn, tag, gt, gb, pk, up_all, gps, gp, wfb, wf, dw, c0, ra1, ra2, rb1, rb2, ze, rz, zh, zr, fin,
    x_ss, x_rs, g_ss, g_rs, t_ss, t_rs, p_ss, p_rs, w_ss, w_rs, v_ss, v_rs, d_ss, d_rs, z_ss, z_rs, f_ss, f_rs, l_sem, word,
):
    feat = x_hbm.shape[0]
    width = w_hbm.shape[0]
    heads = width // (3 * HD)
    d_model = YS * feat
    nz = n_dp // (XS * CORES)
    stride = n_dp // BUNDLES
    scale = 1.0 / math.sqrt(HD)
    norm = 1.0 / math.sqrt(n_dp)
    part = fin.shape[0] // SETS
    half = part // CORES
    sub = half // 2
    q1 = sub // 2
    q2 = q1 // 2
    q3 = q2 // 2
    piece = 2 * q2 // nz

    dp = lax.axis_index("dp")
    me = lax.axis_index("mp")
    right, left, far = (me + 1) % YS, (me + 3) % YS, (me + 2) % YS
    core = dp % CORES
    xi = (dp // CORES) % XS
    zi = dp // (XS * CORES)
    base_xz = zi * (XS * CORES)
    mate = {"dp": dp + 1 - 2 * core}
    even = xi % 2
    near1 = {"dp": base_xz + (xi + 1 - 2 * even) * CORES + core}
    near2 = {"dp": base_xz + ((xi + 3 - 2 * even) % XS) * CORES + core}
    bit1 = ((xi + 1) // 2) % 2
    bit2 = xi // 2

    par, zg = zi % 2, zi // 2
    zn1 = {"dp": dp + (1 - 2 * par) * (XS * CORES)}
    zn2 = {"dp": (dp + n_dp + (2 * par - 1) * (XS * CORES)) % n_dp}

    def z_peer(k):
        return {"dp": ((zi + k) % nz) * (XS * CORES) + xi * CORES + core}

    def remote(src, dst, ss, rs, dev):
        return pltpu.make_async_remote_copy(
            src_ref=src, dst_ref=dst, send_sem=ss, recv_sem=rs,
            device_id=dev, device_id_type=pl.DeviceIdType.MESH,
        )

    def rows(start, size):
        return pl.ds(pl.multiple_of(start, 16), size)

    def order(i):
        return (3 * i) % BUNDLES

    def cols(b):
        return pl.ds(pl.multiple_of(b * CAP, CAP), CAP)

    def g_copy(b):
        off = stride // 2 + b * stride
        to = {"dp": (dp + off) % n_dp}
        return (
            remote(tag.at[b], gt.at[b], t_ss.at[b], t_rs.at[b], to),
            remote(g_hbm.at[:, cols(b)], gb.at[b], g_ss.at[b], g_rs.at[b], to),
        )

    def x_copies(b):
        src = x_hbm.at[:, cols(b)]
        r = rows(me * feat, feat)
        return (
            remote(src, xt.at[b, r], x_ss.at[0, b], x_rs.at[0, b], {"mp": right}),
            remote(src, xt.at[b, r], x_ss.at[1, b], x_rs.at[1, b], {"mp": left}),
        )

    def x_relays(b):
        r = rows(left * feat, feat // 2)
        s = rows(right * feat + feat // 2, feat // 2)
        return (
            remote(xt.at[b, r], xt.at[b, r], x_ss.at[2, b], x_rs.at[2, b], {"mp": right}),
            remote(xt.at[b, s], xt.at[b, s], x_ss.at[3, b], x_rs.at[3, b], {"mp": left}),
        )

    def x_local(b):
        return pltpu.make_async_copy(
            x_hbm.at[:, cols(b)], xt.at[b, rows(me * feat, feat)], l_sem.at[b])

    def p_copies(b):
        r = rows(me * width, width)
        return (
            remote(gp.at[b, r], gp.at[b, r], p_ss.at[0, b], p_rs.at[0, b], {"mp": right}),
            remote(gp.at[b, r], gp.at[b, r], p_ss.at[1, b], p_rs.at[1, b], {"mp": left}),
        )

    def p_relays(b):
        r = rows(left * width, 256)
        s = rows(right * width + 256, width - 256)
        return (
            remote(gp.at[b, r], gp.at[b, r], p_ss.at[2, b], p_rs.at[2, b], {"mp": right}),
            remote(gp.at[b, s], gp.at[b, s], p_ss.at[3, b], p_rs.at[3, b], {"mp": left}),
        )

    fh = feat // CORES

    def w_copy(k):
        to = (me + k) % YS
        return remote(
            wn.at[rows(to * feat + core * fh, fh)], wfb.at[me, rows(core * fh, fh)],
            w_ss.at[k - 1], w_rs.at[k - 1], {"mp": to},
        )

    def v_copy(k):
        who = (me + YS - k) % YS
        r = rows(core * fh, fh)
        return remote(wfb.at[who, r], wfb.at[who, r], v_ss.at[k - 1], v_rs.at[k - 1], mate)

    def spans(s):
        oa = s * part + core * half
        ob = oa + sub
        keep_a, keep_b = oa + bit1 * q1, ob + bit2 * q1
        return oa, ob, keep_a, keep_b, keep_a + bit2 * q2, keep_b + bit1 * q2

    def core_sum(s):
        r = rows(s * part + (1 - core) * half, half)
        return remote(dw.at[r], c0.at[s], d_ss.at[s, 0], d_rs.at[s, 0], mate)

    def x_sum1(s):
        oa, ob = spans(s)[:2]
        ra, rb = rows(oa + (1 - bit1) * q1, q1), rows(ob + (1 - bit2) * q1, q1)
        return (
            remote(dw.at[ra], ra1.at[s], d_ss.at[s, 1], d_rs.at[s, 1], near1),
            remote(dw.at[rb], rb1.at[s], d_ss.at[s, 2], d_rs.at[s, 2], near2),
        )

    def gives(s):
        keep_a, keep_b = spans(s)[2:4]
        return keep_a + (1 - bit2) * q2, keep_b + (1 - bit1) * q2

    def x_sum2(s):
        ga, gb_ = gives(s)
        return (
            remote(dw.at[rows(ga, q2)], ra2.at[s], d_ss.at[s, 3], d_rs.at[s, 3], near2),
            remote(dw.at[rows(gb_, q2)], rb2.at[s], d_ss.at[s, 4], d_rs.at[s, 4], near1),
        )

    def z_half(s):
        give = (1 - par) * q3
        return (
            remote(ze.at[s, rows(give, q3)], rz.at[s, 0:q3], d_ss.at[s, 10], d_rs.at[s, 10], zn1),
            remote(ze.at[s, rows(q2 + give, q3)], rz.at[s, q3:2 * q3], d_ss.at[s, 11], d_rs.at[s, 11], zn2),
        )

    def z_copy(s, k):
        to = ((zi + 2 * k) % nz) // 2
        return remote(zh.at[s, rows(to * piece, piece)], zr.at[s, k], z_ss.at[s, k], z_rs.at[s, k], z_peer(2 * k))

    def spot(s):
        fa, fb = spans(s)[4:]
        at = par * q3 + zg * piece
        return jnp.where(zg < nz // 4, fa + at, fb + at - q3)

    def f_copy(s, k):
        r = rows(spot(s), piece)
        return remote(fin.at[r], fin.at[r], f_ss.at[s, k], f_rs.at[s, k], z_peer(k))

    def same(s, start, size, i, dev):
        r = rows(start, size)
        return remote(fin.at[r], fin.at[r], d_ss.at[s, i], d_rs.at[s, i], dev)

    def x_gather2(s):
        fa, fb = spans(s)[4:]
        return same(s, fa, q2, 5, near2), same(s, fb, q2, 6, near1)

    def x_gather1(s):
        keep_a, keep_b = spans(s)[2:4]
        return same(s, keep_a, q1, 7, near1), same(s, keep_b, q1, 8, near2)

    def core_gather(s):
        return (same(s, s * part + core * half, half, 9, mate),)

    barrier = pltpu.get_barrier_semaphore()
    mesh_id = pl.DeviceIdType.MESH

    for dev in [{"mp": right}, {"mp": left}, mate, near1, near2, zn1, zn2]:
        pl.semaphore_signal(barrier, inc=1, device_id=dev, device_id_type=mesh_id)
    w_local = pltpu.make_async_copy(w_hbm, wt, l_sem.at[BUNDLES])
    w_local.start()
    for i in range(BUNDLES):
        x_local(order(i)).start()

    slot = lax.broadcasted_iota(jnp.int32, (TAG, CAP), 1)
    for b in range(BUNDLES):
        end = counts[b, 0]
        ids = jnp.where(slot >= end, 1, 0)
        for i in range(1, IMGS):
            end = end + counts[b, i]
            ids = ids + jnp.where(slot >= end, 1, 0)
        tag[b] = jnp.where(slot < end, ids - IMGS, slot).astype(F32).astype(BF16)
    for b in range(BUNDLES):
        xt[b, d_model:, :] = jnp.zeros((xt.shape[1] - d_model, CAP), BF16)
    pl.semaphore_wait(barrier, 7)

    def tell(i):
        for k in (2 ** i, nz - 2 ** i):
            pl.semaphore_signal(word.at[i], inc=1, device_id=z_peer(k), device_id_type=mesh_id)

    def hear(i):
        pl.semaphore_wait(word.at[i], 2)

    def start(copies):
        for cp in copies:
            cp.start()

    def arrive(copies):
        for cp in copies:
            cp.wait_recv()

    start(x_copies(0))
    start(x_copies(order(1)))
    tell(0)
    w_local.wait()
    for n in range(d_model // LANES):
        wn[n * LANES:(n + 1) * LANES, :] = wt[:, n * LANES:(n + 1) * LANES].T
    hear(0)
    tell(1)
    start(g_copy(order(0)))
    start(g_copy(order(1)))
    for i in range(BUNDLES):
        x_local(order(i)).wait()
    wfb[me] = wn[rows(me * feat, feat), :]
    hear(1)
    tell(2)

    arrive(x_copies(0))
    start(x_relays(0))
    start(x_copies(order(2)))
    hear(2)
    start(g_copy(order(2)))
    start(g_copy(order(3)))

    mine = rows(me * width, width)
    n_blocks = xt.shape[1] // (2 * LANES)

    def weight_term(n, b):
        return dot(gp[b, mine, :], xt[b, rows(n * 2 * LANES, 2 * LANES), :], ((1,), (1,)))

    def first_blocks(n, _):
        total = weight_term(n, order(0))
        for i in range(1, BUNDLES - 1):
            total += weight_term(n, order(i))
        at = n * 2 * width
        dw[rows(at, width), :] = total[:, :LANES]
        dw[rows(at + width, width), :] = total[:, LANES:]
        return 0

    def bundle(i, _):
        b = order(i)

        @pl.when(i < BUNDLES - 1)
        def _():
            nxt = order(i + 1)
            arrive(x_copies(nxt))
            start(x_relays(nxt))

        @pl.when(i == 0)
        def _():
            start(x_copies(order(3)))

        @pl.when(i == 2)
        def _():
            for k in range(1, YS):
                w_copy(k).start()
            start(p_copies(order(0)))
            start(p_copies(order(1)))

        @pl.when(i == 3)
        def _():
            start(p_copies(order(2)))
            lax.fori_loop(0, n_blocks, first_blocks, 0)

        arrive(x_relays(b))
        pk[...] = dot(wt[...], xt[b, 0:d_model, :], ((1,), (0,)))
        arrive(g_copy(b))
        tags = gt[b].astype(F32)[0:8]
        allowed = tags[0:1, :] == tags.T[:, 0:1]
        up_all[...] = jnp.where(tags[0:1, :] < 0, gb[b].astype(F32), 0.0)
        for h in range(heads):
            o = h * 3 * HD
            query = pk[o:o + HD, :].astype(BF16)
            key = pk[o + HD:o + 2 * HD, :].astype(BF16)
            value = pk[o + 2 * HD:o + 3 * HD, :].astype(BF16)
            up = up_all[h * HD:(h + 1) * HD, :].astype(BF16)
            scores = dot(query, key, ((0,), (0,))) * scale
            masked = jnp.where(allowed, scores, -1e30)
            top = jnp.max(masked, axis=1, keepdims=True)
            exponent = jnp.where(allowed, jnp.exp(masked - top), 0.0)
            probs = exponent * (1.0 / jnp.sum(exponent, axis=1, keepdims=True))
            grad_probs = dot(up, value, ((0,), (0,)))
            row_dot = jnp.sum(probs * grad_probs, axis=1, keepdims=True)
            logits = (probs * (grad_probs - row_dot) * scale).astype(BF16)
            gps[o:o + HD, :] = dot(key, logits, ((1,), (1,)))
            gps[o + HD:o + 2 * HD, :] = dot(query, logits, ((1,), (0,)))
            gps[o + 2 * HD:o + 3 * HD, :] = dot(up, probs.astype(BF16), ((1,), (0,)))
        gp[b, rows(me * width, width), :] = gps[...].astype(BF16)
        return 0

    lax.fori_loop(0, BUNDLES, bundle, 0)
    start(p_copies(order(3)))

    def weight_block(n, _):
        total = weight_term(n, order(BUNDLES - 1))
        at = n * 2 * width
        dw[rows(at, width), :] += total[:, :LANES]
        dw[rows(at + width, width), :] += total[:, LANES:]
        return 0

    for s in range(SETS):
        lax.fori_loop(s * n_blocks // SETS, (s + 1) * n_blocks // SETS, weight_block, 0)
        core_sum(s).start()

    def add_into(at, got, got_at, size):
        dw[rows(at, size), :] += got[rows(got_at, size), :]

    def add_core(s):
        core_sum(s).wait_recv()
        add_into(s * part + core * half, c0.at[s], 0, half)

    def add_x1(s):
        arrive(x_sum1(s))
        ga, gb_ = gives(s)
        fa, fb = spans(s)[4:]
        add_into(ga, ra1.at[s], (1 - bit2) * q2, q2)
        add_into(gb_, rb1.at[s], (1 - bit1) * q2, q2)
        start(x_sum2(s))
        add_into(fa, ra1.at[s], bit2 * q2, q2)
        add_into(fb, rb1.at[s], bit1 * q2, q2)

    def loop_z(f):
        def body(k, _):
            f(k)
            return 0

        lax.fori_loop(1, nz, body, 0)

    def add_x2(s):
        arrive(x_sum2(s))
        fa, fb = spans(s)[4:]
        ze[s, 0:q2, :] = dw[rows(fa, q2), :] + ra2[s]
        ze[s, q2:2 * q2, :] = dw[rows(fb, q2), :] + rb2[s]
        start(z_half(s))

    def loop_zz(f):
        def body(k, _):
            f(k)
            return 0

        lax.fori_loop(1, nz // 2, body, 0)

    def add_z1(s):
        arrive(z_half(s))
        zh[s, 0:q3, :] = ze[s, rows(par * q3, q3), :] + rz[s, 0:q3, :]
        zh[s, q3:2 * q3, :] = ze[s, rows(q2 + par * q3, q3), :] + rz[s, q3:2 * q3, :]
        loop_zz(lambda k: z_copy(s, k).start())

    def add_z(s):
        loop_zz(lambda k: z_copy(s, k).wait_recv())
        total = zh[s, rows(zg * piece, piece), :]
        for k in range(1, nz // 2):
            total += zr[s, k]
        fin[rows(spot(s), piece), :] = (total * norm).astype(BF16)
        loop_z(lambda k: f_copy(s, k).start())

    def pass_on(i):
        arrive(p_copies(order(i)))
        start(p_relays(order(i)))

    def rows_grad(i):
        b = order(i)
        arrive(p_relays(b))
        gx_out[:, b * CAP:(b + 1) * CAP] = dot(wf[...], gp[b], ((1,), (0,))).astype(BF16)

    def gathered_z(s):
        loop_z(lambda k: f_copy(s, k).wait_recv())
        start(x_gather2(s))

    def gathered_x2(s):
        arrive(x_gather2(s))
        start(x_gather1(s))

    def gathered_x1(s):
        arrive(x_gather1(s))
        start(core_gather(s))

    def whole_blocks(s):
        return min(d_model // LANES, s * part // width)

    def gathered_core(s):
        arrive(core_gather(s))
        for n in range(whole_blocks(s), whole_blocks(s + 1)):
            fin_out[:, n * LANES:(n + 1) * LANES] = fin[n * width:(n + 1) * width, :]

    add_core(0)
    start(x_sum1(0))
    add_core(1)
    start(x_sum1(1))
    add_core(2)
    add_x1(0)
    start(x_sum1(2))
    add_x1(1)
    add_x2(0)
    add_x1(2)
    add_z1(0)
    add_x2(1)
    for k in range(1, YS):
        w_copy(k).wait_recv()
        v_copy(k).start()
    add_x2(2)
    add_z1(1)
    add_z1(2)
    pass_on(0)
    pass_on(1)
    for k in range(1, YS):
        v_copy(k).wait_recv()
    for j in range(YS):
        wf[:, j * width:(j + 1) * width] = wfb[j]
    add_z(0)
    pass_on(2)
    add_z(1)
    pass_on(3)
    add_z(2)
    gathered_z(0)
    rows_grad(0)
    gathered_z(1)
    gathered_x2(0)
    rows_grad(1)
    gathered_x1(0)
    gathered_x2(1)
    rows_grad(2)
    gathered_z(2)
    gathered_x1(1)
    gathered_core(0)
    rows_grad(3)
    gathered_x2(2)
    gathered_core(1)
    gathered_x1(2)
    gathered_core(2)

    for b in range(BUNDLES):
        for cp in g_copy(b) + x_copies(b) + x_relays(b) + p_copies(b) + p_relays(b):
            cp.wait_send()
    for k in range(1, YS):
        w_copy(k).wait_send()
        v_copy(k).wait_send()
    for s in range(SETS):
        for cp in x_sum1(s) + x_sum2(s) + z_half(s) + x_gather2(s) + x_gather1(s) + core_gather(s):
            cp.wait_send()
        core_sum(s).wait_send()
        loop_zz(lambda k: z_copy(s, k).wait_send())
        loop_z(lambda k: f_copy(s, k).wait_send())


def shards(patches, counts, qkv_weight, grad_context):
    n_dp = lax.axis_size("dp")
    nz = n_dp // (XS * CORES)
    feat, width, grads = patches.shape[1], qkv_weight.shape[1], grad_context.shape[1]
    d_model = YS * feat
    blocks = d_model // LANES
    parts = n_dp
    unit = -(-(blocks * width) // (parts * SETS * 16)) * SETS * 16
    flat = unit * parts
    wide = 2 * LANES * (-(-blocks // 2))
    half = flat // SETS // CORES
    q1, q2 = half // 4, half // 8
    operands = patches.T, grad_context.T, qkv_weight.T, counts[0]
    dma = pltpu.SemaphoreType.DMA
    hbm_spec = pl.BlockSpec(memory_space=pltpu.HBM)
    gx, fin = pl.pallas_call(
        functools.partial(kernel, n_dp),
        out_shape=(
            jax.ShapeDtypeStruct((feat, SEQ), BF16),
            jax.ShapeDtypeStruct((width, d_model), BF16),
        ),
        in_specs=[hbm_spec] * 3 + [pl.BlockSpec(memory_space=pltpu.SMEM)],
        out_specs=(pl.BlockSpec(memory_space=pltpu.VMEM),) * 2,
        scratch_shapes=[
            pltpu.VMEM((BUNDLES, wide, CAP), BF16),
            pltpu.VMEM((width, d_model), BF16),
            pltpu.VMEM((d_model, width), BF16),
            pltpu.VMEM((BUNDLES, TAG, CAP), BF16),
            pltpu.VMEM((BUNDLES, TAG, CAP), BF16),
            pltpu.VMEM((BUNDLES, grads, CAP), BF16),
            pltpu.VMEM((width, CAP), F32),
            pltpu.VMEM((grads, CAP), F32),
            pltpu.VMEM((width, CAP), F32),
            pltpu.VMEM((BUNDLES, YS * width, CAP), BF16),
            pltpu.VMEM((YS, feat, width), BF16),
            pltpu.VMEM((feat, YS * width), BF16),
            pltpu.VMEM((max(flat, wide // LANES * width), LANES), F32),
            pltpu.VMEM((SETS, half, LANES), F32),
            pltpu.VMEM((SETS, q1, LANES), F32),
            pltpu.VMEM((SETS, q2, LANES), F32),
            pltpu.VMEM((SETS, q1, LANES), F32),
            pltpu.VMEM((SETS, q2, LANES), F32),
            pltpu.VMEM((SETS, 2 * q2, LANES), F32),
            pltpu.VMEM((SETS, q2, LANES), F32),
            pltpu.VMEM((SETS, q2, LANES), F32),
            pltpu.VMEM((SETS, nz // 2, 2 * q2 // nz, LANES), F32),
            pltpu.VMEM((flat, LANES), BF16),
            dma((4, BUNDLES)), dma((4, BUNDLES)),
            dma((BUNDLES,)), dma((BUNDLES,)),
            dma((BUNDLES,)), dma((BUNDLES,)),
            dma((4, BUNDLES)), dma((4, BUNDLES)),
            dma((YS - 1,)), dma((YS - 1,)),
            dma((YS - 1,)), dma((YS - 1,)),
            dma((SETS, 12)), dma((SETS, 12)),
            dma((SETS, nz // 2)), dma((SETS, nz // 2)),
            dma((SETS, nz)), dma((SETS, nz)),
            dma((BUNDLES + 1,)),
            pltpu.SemaphoreType.REGULAR((3,)),
        ],
        compiler_params=pltpu.CompilerParams(
            collective_id=0, has_side_effects=True, vmem_limit_bytes=50 * 1024 * 1024),
        name="layer",
    )(*[pltpu.with_memory_space_constraint(a, pltpu.HBM) for a in operands])
    return gx.T, fin.T


def solution(mesh):
    in_specs = (P("dp", "mp"), P("dp", None, None), P(None, "mp"), P("dp", "mp"))
    out_specs = (P("dp", "mp"), P(None, "mp"))
    return jax.shard_map(shards, mesh=mesh, in_specs=in_specs, out_specs=out_specs, check_vma=False)
```

```python
import functools
import math

import jax
import jax.numpy as jnp
from jax import lax
from jax.experimental import pallas as pl
from jax.experimental.pallas import tpu as pltpu
from jax.sharding import PartitionSpec as P

HD = 88
IMGS = 4
BUNDLES = 4
CAP = 256
SEQ = 1024
YS = 4
XS = 4
CORES = 2
LANES = 128
SETS = 3
TAG = 16

F32 = jnp.float32
BF16 = jnp.bfloat16


def dot(a, b, dims):
    return lax.dot_general(a, b, (dims, ((), ())), preferred_element_type=F32)


def kernel(
    n_dp,
    x_hbm, g_hbm, w_hbm, counts,
    gx_out, fin_out,
    xt, wt, wn, tag, gt, gb, pk, up_all, gps, gp, wfb, wf, dw, c0, ra1, ra2, rb1, rb2, ze, rz, zh, zr, fin,
    x_ss, x_rs, g_ss, g_rs, t_ss, t_rs, p_ss, p_rs, w_ss, w_rs, v_ss, v_rs, d_ss, d_rs, z_ss, z_rs, f_ss, f_rs, l_sem, word,
):
    feat = x_hbm.shape[0]
    width = w_hbm.shape[0]
    heads = width // (3 * HD)
    d_model = YS * feat
    nz = n_dp // (XS * CORES)
    stride = n_dp // BUNDLES
    scale = 1.0 / math.sqrt(HD)
    norm = 1.0 / math.sqrt(n_dp)
    part = fin.shape[0] // SETS
    half = part // CORES
    sub = half // 2
    q1 = sub // 2
    q2 = q1 // 2
    q3 = q2 // 2
    piece = 2 * q2 // nz

    dp = lax.axis_index("dp")
    me = lax.axis_index("mp")
    right, left, far = (me + 1) % YS, (me + 3) % YS, (me + 2) % YS
    core = dp % CORES
    xi = (dp // CORES) % XS
    zi = dp // (XS * CORES)
    base_xz = zi * (XS * CORES)
    mate = {"dp": dp + 1 - 2 * core}
    even = xi % 2
    near1 = {"dp": base_xz + (xi + 1 - 2 * even) * CORES + core}
    near2 = {"dp": base_xz + ((xi + 3 - 2 * even) % XS) * CORES + core}
    bit1 = ((xi + 1) // 2) % 2
    bit2 = xi // 2

    par, zg = zi % 2, zi // 2
    zn1 = {"dp": dp + (1 - 2 * par) * (XS * CORES)}
    zn2 = {"dp": (dp + n_dp + (2 * par - 1) * (XS * CORES)) % n_dp}

    def z_peer(k):
        return {"dp": ((zi + k) % nz) * (XS * CORES) + xi * CORES + core}

    def remote(src, dst, ss, rs, dev):
        return pltpu.make_async_remote_copy(
            src_ref=src, dst_ref=dst, send_sem=ss, recv_sem=rs,
            device_id=dev, device_id_type=pl.DeviceIdType.MESH,
        )

    def rows(start, size):
        return pl.ds(pl.multiple_of(start, 16), size)

    def order(i):
        return (3 * i) % BUNDLES

    def cols(b):
        return pl.ds(pl.multiple_of(b * CAP, CAP), CAP)

    def g_copy(b):
        off = stride // 2 + b * stride
        to = {"dp": (dp + off) % n_dp}
        return (
            remote(tag.at[b], gt.at[b], t_ss.at[b], t_rs.at[b], to),
            remote(g_hbm.at[:, cols(b)], gb.at[b], g_ss.at[b], g_rs.at[b], to),
        )

    def x_copies(b):
        src = x_hbm.at[:, cols(b)]
        r = rows(me * feat, feat)
        return (
            remote(src, xt.at[b, r], x_ss.at[0, b], x_rs.at[0, b], {"mp": right}),
            remote(src, xt.at[b, r], x_ss.at[1, b], x_rs.at[1, b], {"mp": left}),
        )

    def x_relays(b):
        r = rows(left * feat, feat // 2)
        s = rows(right * feat + feat // 2, feat // 2)
        return (
            remote(xt.at[b, r], xt.at[b, r], x_ss.at[2, b], x_rs.at[2, b], {"mp": right}),
            remote(xt.at[b, s], xt.at[b, s], x_ss.at[3, b], x_rs.at[3, b], {"mp": left}),
        )

    def x_local(b):
        return pltpu.make_async_copy(
            x_hbm.at[:, cols(b)], xt.at[b, rows(me * feat, feat)], l_sem.at[b])

    def p_copies(b):
        r = rows(me * width, width)
        return (
            remote(gp.at[b, r], gp.at[b, r], p_ss.at[0, b], p_rs.at[0, b], {"mp": right}),
            remote(gp.at[b, r], gp.at[b, r], p_ss.at[1, b], p_rs.at[1, b], {"mp": left}),
        )

    def p_relays(b):
        r = rows(left * width, 256)
        s = rows(right * width + 256, width - 256)
        return (
            remote(gp.at[b, r], gp.at[b, r], p_ss.at[2, b], p_rs.at[2, b], {"mp": right}),
            remote(gp.at[b, s], gp.at[b, s], p_ss.at[3, b], p_rs.at[3, b], {"mp": left}),
        )

    fh = feat // CORES

    def w_copy(k):
        to = (me + k) % YS
        return remote(
            wn.at[rows(to * feat + core * fh, fh)], wfb.at[me, rows(core * fh, fh)],
            w_ss.at[k - 1], w_rs.at[k - 1], {"mp": to},
        )

    def v_copy(k):
        who = (me + YS - k) % YS
        r = rows(core * fh, fh)
        return remote(wfb.at[who, r], wfb.at[who, r], v_ss.at[k - 1], v_rs.at[k - 1], mate)

    def spans(s):
        oa = s * part + core * half
        ob = oa + sub
        keep_a, keep_b = oa + bit1 * q1, ob + bit2 * q1
        return oa, ob, keep_a, keep_b, keep_a + bit2 * q2, keep_b + bit1 * q2

    def core_sum(s):
        r = rows(s * part + (1 - core) * half, half)
        return remote(dw.at[r], c0.at[s], d_ss.at[s, 0], d_rs.at[s, 0], mate)

    def x_sum1(s):
        oa, ob = spans(s)[:2]
        ra, rb = rows(oa + (1 - bit1) * q1, q1), rows(ob + (1 - bit2) * q1, q1)
        return (
            remote(dw.at[ra], ra1.at[s], d_ss.at[s, 1], d_rs.at[s, 1], near1),
            remote(dw.at[rb], rb1.at[s], d_ss.at[s, 2], d_rs.at[s, 2], near2),
        )

    def gives(s):
        keep_a, keep_b = spans(s)[2:4]
        return keep_a + (1 - bit2) * q2, keep_b + (1 - bit1) * q2

    def x_sum2(s):
        ga, gb_ = gives(s)
        return (
            remote(dw.at[rows(ga, q2)], ra2.at[s], d_ss.at[s, 3], d_rs.at[s, 3], near2),
            remote(dw.at[rows(gb_, q2)], rb2.at[s], d_ss.at[s, 4], d_rs.at[s, 4], near1),
        )

    def z_half(s):
        give = (1 - par) * q3
        return (
            remote(ze.at[s, rows(give, q3)], rz.at[s, 0:q3], d_ss.at[s, 10], d_rs.at[s, 10], zn1),
            remote(ze.at[s, rows(q2 + give, q3)], rz.at[s, q3:2 * q3], d_ss.at[s, 11], d_rs.at[s, 11], zn2),
        )

    def z_copy(s, k):
        to = ((zi + 2 * k) % nz) // 2
        return remote(zh.at[s, rows(to * piece, piece)], zr.at[s, k], z_ss.at[s, k], z_rs.at[s, k], z_peer(2 * k))

    def spot(s):
        fa, fb = spans(s)[4:]
        at = par * q3 + zg * piece
        return jnp.where(zg < nz // 4, fa + at, fb + at - q3)

    def f_copy(s, k):
        r = rows(spot(s), piece)
        return remote(fin.at[r], fin.at[r], f_ss.at[s, k], f_rs.at[s, k], z_peer(k))

    def same(s, start, size, i, dev):
        r = rows(start, size)
        return remote(fin.at[r], fin.at[r], d_ss.at[s, i], d_rs.at[s, i], dev)

    def x_gather2(s):
        fa, fb = spans(s)[4:]
        return same(s, fa, q2, 5, near2), same(s, fb, q2, 6, near1)

    def x_gather1(s):
        keep_a, keep_b = spans(s)[2:4]
        return same(s, keep_a, q1, 7, near1), same(s, keep_b, q1, 8, near2)

    def core_gather(s):
        return (same(s, s * part + core * half, half, 9, mate),)

    barrier = pltpu.get_barrier_semaphore()
    mesh_id = pl.DeviceIdType.MESH

    for dev in [{"mp": right}, {"mp": left}, mate, near1, near2, zn1, zn2]:
        pl.semaphore_signal(barrier, inc=1, device_id=dev, device_id_type=mesh_id)
    w_local = pltpu.make_async_copy(w_hbm, wt, l_sem.at[BUNDLES])
    w_local.start()
    for i in range(BUNDLES):
        x_local(order(i)).start()

    slot = lax.broadcasted_iota(jnp.int32, (TAG, CAP), 1)
    for b in range(BUNDLES):
        end = counts[b, 0]
        ids = jnp.where(slot >= end, 1, 0)
        for i in range(1, IMGS):
            end = end + counts[b, i]
            ids = ids + jnp.where(slot >= end, 1, 0)
        tag[b] = jnp.where(slot < end, ids - IMGS, slot).astype(F32).astype(BF16)
    for b in range(BUNDLES):
        xt[b, d_model:, :] = jnp.zeros((xt.shape[1] - d_model, CAP), BF16)
    pl.semaphore_wait(barrier, 7)

    def tell(i):
        for k in (2 ** i, nz - 2 ** i):
            pl.semaphore_signal(word.at[i], inc=1, device_id=z_peer(k), device_id_type=mesh_id)

    def hear(i):
        pl.semaphore_wait(word.at[i], 2)

    def start(copies):
        for cp in copies:
            cp.start()

    def arrive(copies):
        for cp in copies:
            cp.wait_recv()

    start(x_copies(0))
    start(x_copies(order(1)))
    tell(0)
    w_local.wait()
    for n in range(d_model // LANES):
        wn[n * LANES:(n + 1) * LANES, :] = wt[:, n * LANES:(n + 1) * LANES].T
    hear(0)
    tell(1)
    start(g_copy(order(0)))
    start(g_copy(order(1)))
    for i in range(BUNDLES):
        x_local(order(i)).wait()
    wfb[me] = wn[rows(me * feat, feat), :]
    hear(1)
    tell(2)

    arrive(x_copies(0))
    start(x_relays(0))
    start(x_copies(order(2)))
    hear(2)
    start(g_copy(order(2)))
    start(g_copy(order(3)))

    mine = rows(me * width, width)
    n_blocks = xt.shape[1] // (2 * LANES)

    def weight_term(n, b):
        return dot(gp[b, mine, :], xt[b, rows(n * 2 * LANES, 2 * LANES), :], ((1,), (1,)))

    def first_blocks(n, _):
        total = weight_term(n, order(0))
        for i in range(1, BUNDLES - 1):
            total += weight_term(n, order(i))
        at = n * 2 * width
        dw[rows(at, width), :] = total[:, :LANES]
        dw[rows(at + width, width), :] = total[:, LANES:]
        return 0

    def bundle(i, _):
        b = order(i)

        @pl.when(i < BUNDLES - 1)
        def _():
            nxt = order(i + 1)
            arrive(x_copies(nxt))
            start(x_relays(nxt))

        @pl.when(i == 0)
        def _():
            start(x_copies(order(3)))

        @pl.when(i == 2)
        def _():
            for k in range(1, YS):
                w_copy(k).start()
            start(p_copies(order(0)))
            start(p_copies(order(1)))

        @pl.when(i == 3)
        def _():
            start(p_copies(order(2)))
            lax.fori_loop(0, n_blocks, first_blocks, 0)

        arrive(x_relays(b))
        pk[...] = dot(wt[...], xt[b, 0:d_model, :], ((1,), (0,)))
        arrive(g_copy(b))
        tags = gt[b].astype(F32)[0:8]
        allowed = tags[0:1, :] == tags.T[:, 0:1]
        up_all[...] = jnp.where(tags[0:1, :] < 0, gb[b].astype(F32), 0.0)
        for h in range(heads):
            o = h * 3 * HD
            query = pk[o:o + HD, :].astype(BF16)
            key = pk[o + HD:o + 2 * HD, :].astype(BF16)
            value = pk[o + 2 * HD:o + 3 * HD, :].astype(BF16)
            up = up_all[h * HD:(h + 1) * HD, :].astype(BF16)
            scores = dot(query, key, ((0,), (0,))) * scale
            masked = jnp.where(allowed, scores, -1e30)
            top = jnp.max(masked, axis=1, keepdims=True)
            exponent = jnp.where(allowed, jnp.exp(masked - top), 0.0)
            probs = exponent * (1.0 / jnp.sum(exponent, axis=1, keepdims=True))
            grad_probs = dot(up, value, ((0,), (0,)))
            row_dot = jnp.sum(probs * grad_probs, axis=1, keepdims=True)
            logits = (probs * (grad_probs - row_dot) * scale).astype(BF16)
            gps[o:o + HD, :] = dot(key, logits, ((1,), (1,)))
            gps[o + HD:o + 2 * HD, :] = dot(query, logits, ((1,), (0,)))
            gps[o + 2 * HD:o + 3 * HD, :] = dot(up, probs.astype(BF16), ((1,), (0,)))
        gp[b, rows(me * width, width), :] = gps[...].astype(BF16)
        return 0

    lax.fori_loop(0, BUNDLES, bundle, 0)
    start(p_copies(order(3)))

    def weight_block(n, _):
        total = weight_term(n, order(BUNDLES - 1))
        at = n * 2 * width
        dw[rows(at, width), :] += total[:, :LANES]
        dw[rows(at + width, width), :] += total[:, LANES:]
        return 0

    for s in range(SETS):
        lax.fori_loop(s * n_blocks // SETS, (s + 1) * n_blocks // SETS, weight_block, 0)
        core_sum(s).start()

    def add_into(at, got, got_at, size):
        dw[rows(at, size), :] += got[rows(got_at, size), :]

    def add_core(s):
        core_sum(s).wait_recv()
        add_into(s * part + core * half, c0.at[s], 0, half)

    def add_x1(s):
        arrive(x_sum1(s))
        ga, gb_ = gives(s)
        fa, fb = spans(s)[4:]
        add_into(ga, ra1.at[s], (1 - bit2) * q2, q2)
        add_into(gb_, rb1.at[s], (1 - bit1) * q2, q2)
        start(x_sum2(s))
        add_into(fa, ra1.at[s], bit2 * q2, q2)
        add_into(fb, rb1.at[s], bit1 * q2, q2)

    def loop_z(f):
        def body(k, _):
            f(k)
            return 0

        lax.fori_loop(1, nz, body, 0)

    def add_x2(s):
        arrive(x_sum2(s))
        fa, fb = spans(s)[4:]
        ze[s, 0:q2, :] = dw[rows(fa, q2), :] + ra2[s]
        ze[s, q2:2 * q2, :] = dw[rows(fb, q2), :] + rb2[s]
        start(z_half(s))

    def loop_zz(f):
        def body(k, _):
            f(k)
            return 0

        lax.fori_loop(1, nz // 2, body, 0)

    def add_z1(s):
        arrive(z_half(s))
        zh[s, 0:q3, :] = ze[s, rows(par * q3, q3), :] + rz[s, 0:q3, :]
        zh[s, q3:2 * q3, :] = ze[s, rows(q2 + par * q3, q3), :] + rz[s, q3:2 * q3, :]
        loop_zz(lambda k: z_copy(s, k).start())

    def add_z(s):
        loop_zz(lambda k: z_copy(s, k).wait_recv())
        total = zh[s, rows(zg * piece, piece), :]
        for k in range(1, nz // 2):
            total += zr[s, k]
        fin[rows(spot(s), piece), :] = (total * norm).astype(BF16)
        loop_z(lambda k: f_copy(s, k).start())

    def pass_on(i):
        arrive(p_copies(order(i)))
        start(p_relays(order(i)))

    def rows_grad(i):
        b = order(i)
        arrive(p_relays(b))
        gx_out[:, b * CAP:(b + 1) * CAP] = dot(wf[...], gp[b], ((1,), (0,))).astype(BF16)

    def gathered_z(s):
        loop_z(lambda k: f_copy(s, k).wait_recv())
        start(x_gather2(s))

    def gathered_x2(s):
        arrive(x_gather2(s))
        start(x_gather1(s))

    def gathered_x1(s):
        arrive(x_gather1(s))
        start(core_gather(s))

    def whole_blocks(s):
        return min(d_model // LANES, s * part // width)

    def gathered_core(s):
        arrive(core_gather(s))
        for n in range(whole_blocks(s), whole_blocks(s + 1)):
            fin_out[:, n * LANES:(n + 1) * LANES] = fin[n * width:(n + 1) * width, :]

    add_core(0)
    start(x_sum1(0))
    add_core(1)
    start(x_sum1(1))
    add_core(2)
    add_x1(0)
    start(x_sum1(2))
    add_x1(1)
    add_x2(0)
    add_x1(2)
    add_z1(0)
    add_x2(1)
    for k in range(1, YS):
        w_copy(k).wait_recv()
        v_copy(k).start()
    add_x2(2)
    add_z1(1)
    add_z1(2)
    pass_on(0)
    pass_on(1)
    for k in range(1, YS):
        v_copy(k).wait_recv()
    for j in range(YS):
        wf[:, j * width:(j + 1) * width] = wfb[j]
    add_z(0)
    pass_on(2)
    add_z(1)
    pass_on(3)
    add_z(2)
    gathered_z(0)
    rows_grad(0)
    gathered_z(1)
    gathered_x2(0)
    rows_grad(1)
    gathered_z(2)
    gathered_x2(1)
    rows_grad(2)
    gathered_x1(0)
    gathered_x2(2)
    rows_grad(3)
    gathered_x1(1)
    gathered_core(0)
    gathered_x1(2)
    gathered_core(1)
    gathered_core(2)

    for b in range(BUNDLES):
        for cp in g_copy(b) + x_copies(b) + x_relays(b) + p_copies(b) + p_relays(b):
            cp.wait_send()
    for k in range(1, YS):
        w_copy(k).wait_send()
        v_copy(k).wait_send()
    for s in range(SETS):
        for cp in x_sum1(s) + x_sum2(s) + z_half(s) + x_gather2(s) + x_gather1(s) + core_gather(s):
            cp.wait_send()
        core_sum(s).wait_send()
        loop_zz(lambda k: z_copy(s, k).wait_send())
        loop_z(lambda k: f_copy(s, k).wait_send())


def shards(patches, counts, qkv_weight, grad_context):
    n_dp = lax.axis_size("dp")
    nz = n_dp // (XS * CORES)
    feat, width, grads = patches.shape[1], qkv_weight.shape[1], grad_context.shape[1]
    d_model = YS * feat
    blocks = d_model // LANES
    parts = n_dp
    unit = -(-(blocks * width) // (parts * SETS * 16)) * SETS * 16
    flat = unit * parts
    wide = 2 * LANES * (-(-blocks // 2))
    half = flat // SETS // CORES
    q1, q2 = half // 4, half // 8
    operands = patches.T, grad_context.T, qkv_weight.T, counts[0]
    dma = pltpu.SemaphoreType.DMA
    hbm_spec = pl.BlockSpec(memory_space=pltpu.HBM)
    gx, fin = pl.pallas_call(
        functools.partial(kernel, n_dp),
        out_shape=(
            jax.ShapeDtypeStruct((feat, SEQ), BF16),
            jax.ShapeDtypeStruct((width, d_model), BF16),
        ),
        in_specs=[hbm_spec] * 3 + [pl.BlockSpec(memory_space=pltpu.SMEM)],
        out_specs=(pl.BlockSpec(memory_space=pltpu.VMEM),) * 2,
        scratch_shapes=[
            pltpu.VMEM((BUNDLES, wide, CAP), BF16),
            pltpu.VMEM((width, d_model), BF16),
            pltpu.VMEM((d_model, width), BF16),
            pltpu.VMEM((BUNDLES, TAG, CAP), BF16),
            pltpu.VMEM((BUNDLES, TAG, CAP), BF16),
            pltpu.VMEM((BUNDLES, grads, CAP), BF16),
            pltpu.VMEM((width, CAP), F32),
            pltpu.VMEM((grads, CAP), F32),
            pltpu.VMEM((width, CAP), F32),
            pltpu.VMEM((BUNDLES, YS * width, CAP), BF16),
            pltpu.VMEM((YS, feat, width), BF16),
            pltpu.VMEM((feat, YS * width), BF16),
            pltpu.VMEM((max(flat, wide // LANES * width), LANES), F32),
            pltpu.VMEM((SETS, half, LANES), F32),
            pltpu.VMEM((SETS, q1, LANES), F32),
            pltpu.VMEM((SETS, q2, LANES), F32),
            pltpu.VMEM((SETS, q1, LANES), F32),
            pltpu.VMEM((SETS, q2, LANES), F32),
            pltpu.VMEM((SETS, 2 * q2, LANES), F32),
            pltpu.VMEM((SETS, q2, LANES), F32),
            pltpu.VMEM((SETS, q2, LANES), F32),
            pltpu.VMEM((SETS, nz // 2, 2 * q2 // nz, LANES), F32),
            pltpu.VMEM((flat, LANES), BF16),
            dma((4, BUNDLES)), dma((4, BUNDLES)),
            dma((BUNDLES,)), dma((BUNDLES,)),
            dma((BUNDLES,)), dma((BUNDLES,)),
            dma((4, BUNDLES)), dma((4, BUNDLES)),
            dma((YS - 1,)), dma((YS - 1,)),
            dma((YS - 1,)), dma((YS - 1,)),
            dma((SETS, 12)), dma((SETS, 12)),
            dma((SETS, nz // 2)), dma((SETS, nz // 2)),
            dma((SETS, nz)), dma((SETS, nz)),
            dma((BUNDLES + 1,)),
            pltpu.SemaphoreType.REGULAR((3,)),
        ],
        compiler_params=pltpu.CompilerParams(
            collective_id=0, has_side_effects=True, vmem_limit_bytes=50 * 1024 * 1024),
        name="layer",
    )(*[pltpu.with_memory_space_constraint(a, pltpu.HBM) for a in operands])
    return gx.T, fin.T


def solution(mesh):
    in_specs = (P("dp", "mp"), P("dp", None, None), P(None, "mp"), P("dp", "mp"))
    out_specs = (P("dp", "mp"), P(None, "mp"))
    return jax.shard_map(shards, mesh=mesh, in_specs=in_specs, out_specs=out_specs, check_vma=False)
```

```python
import functools
import math

import jax
import jax.numpy as jnp
from jax import lax
from jax.experimental import pallas as pl
from jax.experimental.pallas import tpu as pltpu
from jax.sharding import PartitionSpec as P

HD = 88
IMGS = 4
BUNDLES = 4
CAP = 256
SEQ = 1024
YS = 4
XS = 4
CORES = 2
LANES = 128
SETS = 3
TAG = 16

F32 = jnp.float32
BF16 = jnp.bfloat16


def dot(a, b, dims):
    return lax.dot_general(a, b, (dims, ((), ())), preferred_element_type=F32)


def kernel(
    n_dp,
    x_hbm, g_hbm, w_hbm, counts,
    gx_out, fin_out,
    xt, wt, wn, tag, gt, gb, pk, up_all, gps, gp, wfb, wf, dw, c0, ra1, ra2, rb1, rb2, ze, rz, zh, zf, zr, fin,
    x_ss, x_rs, g_ss, g_rs, t_ss, t_rs, p_ss, p_rs, w_ss, w_rs, v_ss, v_rs, d_ss, d_rs, z_ss, z_rs, f_ss, f_rs, l_sem, word,
):
    feat = x_hbm.shape[0]
    width = w_hbm.shape[0]
    heads = width // (3 * HD)
    d_model = YS * feat
    nz = n_dp // (XS * CORES)
    stride = n_dp // BUNDLES
    scale = 1.0 / math.sqrt(HD)
    norm = 1.0 / math.sqrt(n_dp)
    part = fin.shape[0] // SETS
    half = part // CORES
    sub = half // 2
    q1 = sub // 2
    q2 = q1 // 2
    q3 = q2 // 2
    piece = 2 * q2 // nz

    dp = lax.axis_index("dp")
    me = lax.axis_index("mp")
    right, left, far = (me + 1) % YS, (me + 3) % YS, (me + 2) % YS
    core = dp % CORES
    xi = (dp // CORES) % XS
    zi = dp // (XS * CORES)
    base_xz = zi * (XS * CORES)
    mate = {"dp": dp + 1 - 2 * core}
    even = xi % 2
    near1 = {"dp": base_xz + (xi + 1 - 2 * even) * CORES + core}
    near2 = {"dp": base_xz + ((xi + 3 - 2 * even) % XS) * CORES + core}
    bit1 = ((xi + 1) // 2) % 2
    bit2 = xi // 2

    par, zg = zi % 2, zi // 2
    zn1 = {"dp": dp + (1 - 2 * par) * (XS * CORES)}
    zn2 = {"dp": (dp + n_dp + (2 * par - 1) * (XS * CORES)) % n_dp}

    def z_peer(k):
        return {"dp": ((zi + k) % nz) * (XS * CORES) + xi * CORES + core}

    def remote(src, dst, ss, rs, dev):
        return pltpu.make_async_remote_copy(
            src_ref=src, dst_ref=dst, send_sem=ss, recv_sem=rs,
            device_id=dev, device_id_type=pl.DeviceIdType.MESH,
        )

    def rows(start, size):
        return pl.ds(pl.multiple_of(start, 16), size)

    def order(i):
        return (3 * i) % BUNDLES

    def cols(b):
        return pl.ds(pl.multiple_of(b * CAP, CAP), CAP)

    def g_copy(b):
        off = stride // 2 + b * stride
        to = {"dp": (dp + off) % n_dp}
        return (
            remote(tag.at[b], gt.at[b], t_ss.at[b], t_rs.at[b], to),
            remote(g_hbm.at[:, cols(b)], gb.at[b], g_ss.at[b], g_rs.at[b], to),
        )

    def x_copies(b):
        src = x_hbm.at[:, cols(b)]
        r = rows(me * feat, feat)
        return (
            remote(src, xt.at[b, r], x_ss.at[0, b], x_rs.at[0, b], {"mp": right}),
            remote(src, xt.at[b, r], x_ss.at[1, b], x_rs.at[1, b], {"mp": left}),
        )

    def x_relays(b):
        r = rows(left * feat, feat // 2)
        s = rows(right * feat + feat // 2, feat // 2)
        return (
            remote(xt.at[b, r], xt.at[b, r], x_ss.at[2, b], x_rs.at[2, b], {"mp": right}),
            remote(xt.at[b, s], xt.at[b, s], x_ss.at[3, b], x_rs.at[3, b], {"mp": left}),
        )

    def x_local(b):
        return pltpu.make_async_copy(
            x_hbm.at[:, cols(b)], xt.at[b, rows(me * feat, feat)], l_sem.at[b])

    def p_copies(b):
        r = rows(me * width, width)
        return (
            remote(gp.at[b, r], gp.at[b, r], p_ss.at[0, b], p_rs.at[0, b], {"mp": right}),
            remote(gp.at[b, r], gp.at[b, r], p_ss.at[1, b], p_rs.at[1, b], {"mp": left}),
        )

    def p_relays(b):
        r = rows(left * width, 256)
        s = rows(right * width + 256, width - 256)
        return (
            remote(gp.at[b, r], gp.at[b, r], p_ss.at[2, b], p_rs.at[2, b], {"mp": right}),
            remote(gp.at[b, s], gp.at[b, s], p_ss.at[3, b], p_rs.at[3, b], {"mp": left}),
        )

    fh = feat // CORES

    def w_copy(k):
        to = (me + k) % YS
        return remote(
            wn.at[rows(to * feat + core * fh, fh)], wfb.at[me, rows(core * fh, fh)],
            w_ss.at[k - 1], w_rs.at[k - 1], {"mp": to},
        )

    def v_copy(k):
        who = (me + YS - k) % YS
        r = rows(core * fh, fh)
        return remote(wfb.at[who, r], wfb.at[who, r], v_ss.at[k - 1], v_rs.at[k - 1], mate)

    def spans(s):
        oa = s * part + core * half
        ob = oa + sub
        keep_a, keep_b = oa + bit1 * q1, ob + bit2 * q1
        return oa, ob, keep_a, keep_b, keep_a + bit2 * q2, keep_b + bit1 * q2

    def core_sum(s):
        r = rows(s * part + (1 - core) * half, half)
        return remote(dw.at[r], c0.at[s], d_ss.at[s, 0], d_rs.at[s, 0], mate)

    def x_sum1(s):
        oa, ob = spans(s)[:2]
        ra, rb = rows(oa + (1 - bit1) * q1, q1), rows(ob + (1 - bit2) * q1, q1)
        return (
            remote(dw.at[ra], ra1.at[s], d_ss.at[s, 1], d_rs.at[s, 1], near1),
            remote(dw.at[rb], rb1.at[s], d_ss.at[s, 2], d_rs.at[s, 2], near2),
        )

    def gives(s):
        keep_a, keep_b = spans(s)[2:4]
        return keep_a + (1 - bit2) * q2, keep_b + (1 - bit1) * q2

    def x_sum2(s):
        ga, gb_ = gives(s)
        return (
            remote(dw.at[rows(ga, q2)], ra2.at[s], d_ss.at[s, 3], d_rs.at[s, 3], near2),
            remote(dw.at[rows(gb_, q2)], rb2.at[s], d_ss.at[s, 4], d_rs.at[s, 4], near1),
        )

    def z_half(s):
        give = (1 - par) * q3
        return (
            remote(ze.at[s, rows(give, q3)], rz.at[s, 0:q3], d_ss.at[s, 10], d_rs.at[s, 10], zn1),
            remote(ze.at[s, rows(q2 + give, q3)], rz.at[s, q3:2 * q3], d_ss.at[s, 11], d_rs.at[s, 11], zn2),
        )

    def z_copy(s, k):
        to = ((zi + 2 * k) % nz) // 2
        return remote(zh.at[s, rows(to * piece, piece)], zr.at[s, k], z_ss.at[s, k], z_rs.at[s, k], z_peer(2 * k))

    def far_copy(s):
        to = ((zi + nz // 2) % nz) // 2
        return remote(zh.at[s, rows(to * piece, piece)], zf.at[s], d_ss.at[s, 12], d_rs.at[s, 12], z_peer(nz - nz // 4))

    direct = [k for k in range(1, nz // 2) if k not in (nz // 4, nz // 2 - nz // 8)]
    last = nz // 2 - nz // 8

    def spot(s):
        fa, fb = spans(s)[4:]
        at = par * q3 + zg * piece
        return jnp.where(zg < nz // 4, fa + at, fb + at - q3)

    def f_copy(s, k):
        r = rows(spot(s), piece)
        return remote(fin.at[r], fin.at[r], f_ss.at[s, k], f_rs.at[s, k], z_peer(k))

    def same(s, start, size, i, dev):
        r = rows(start, size)
        return remote(fin.at[r], fin.at[r], d_ss.at[s, i], d_rs.at[s, i], dev)

    def x_gather2(s):
        fa, fb = spans(s)[4:]
        return same(s, fa, q2, 5, near2), same(s, fb, q2, 6, near1)

    def x_gather1(s):
        keep_a, keep_b = spans(s)[2:4]
        return same(s, keep_a, q1, 7, near1), same(s, keep_b, q1, 8, near2)

    def core_gather(s):
        return (same(s, s * part + core * half, half, 9, mate),)

    barrier = pltpu.get_barrier_semaphore()
    mesh_id = pl.DeviceIdType.MESH

    for dev in [{"mp": right}, {"mp": left}, mate, near1, near2, zn1, zn2]:
        pl.semaphore_signal(barrier, inc=1, device_id=dev, device_id_type=mesh_id)
    w_local = pltpu.make_async_copy(w_hbm, wt, l_sem.at[BUNDLES])
    w_local.start()
    for i in range(BUNDLES):
        x_local(order(i)).start()

    slot = lax.broadcasted_iota(jnp.int32, (TAG, CAP), 1)
    for b in range(BUNDLES):
        end = counts[b, 0]
        ids = jnp.where(slot >= end, 1, 0)
        for i in range(1, IMGS):
            end = end + counts[b, i]
            ids = ids + jnp.where(slot >= end, 1, 0)
        tag[b] = jnp.where(slot < end, ids - IMGS, slot).astype(F32).astype(BF16)
    for b in range(BUNDLES):
        xt[b, d_model:, :] = jnp.zeros((xt.shape[1] - d_model, CAP), BF16)
    pl.semaphore_wait(barrier, 7)

    def tell(i):
        for k in (2 ** i, nz - 2 ** i):
            pl.semaphore_signal(word.at[i], inc=1, device_id=z_peer(k), device_id_type=mesh_id)

    def hear(i):
        pl.semaphore_wait(word.at[i], 2)

    def start(copies):
        for cp in copies:
            cp.start()

    def arrive(copies):
        for cp in copies:
            cp.wait_recv()

    start(x_copies(0))
    start(x_copies(order(1)))
    tell(0)
    w_local.wait()
    for n in range(d_model // LANES):
        wn[n * LANES:(n + 1) * LANES, :] = wt[:, n * LANES:(n + 1) * LANES].T
    hear(0)
    tell(1)
    start(g_copy(order(0)))
    start(g_copy(order(1)))
    for i in range(BUNDLES):
        x_local(order(i)).wait()
    wfb[me] = wn[rows(me * feat, feat), :]
    hear(1)
    tell(2)

    arrive(x_copies(0))
    start(x_relays(0))
    start(x_copies(order(2)))
    hear(2)
    start(g_copy(order(2)))
    start(g_copy(order(3)))

    mine = rows(me * width, width)
    n_blocks = xt.shape[1] // (2 * LANES)

    def weight_term(n, b):
        return dot(gp[b, mine, :], xt[b, rows(n * 2 * LANES, 2 * LANES), :], ((1,), (1,)))

    def first_blocks(n, _):
        total = weight_term(n, order(0))
        for i in range(1, BUNDLES - 1):
            total += weight_term(n, order(i))
        at = n * 2 * width
        dw[rows(at, width), :] = total[:, :LANES]
        dw[rows(at + width, width), :] = total[:, LANES:]
        return 0

    def bundle(i, _):
        b = order(i)

        @pl.when(i < BUNDLES - 1)
        def _():
            nxt = order(i + 1)
            arrive(x_copies(nxt))
            start(x_relays(nxt))

        @pl.when(i == 0)
        def _():
            start(x_copies(order(3)))

        @pl.when(i == 2)
        def _():
            for k in range(1, YS):
                w_copy(k).start()
            start(p_copies(order(0)))
            start(p_copies(order(1)))

        @pl.when(i == 3)
        def _():
            start(p_copies(order(2)))
            lax.fori_loop(0, n_blocks, first_blocks, 0)

        arrive(x_relays(b))
        pk[...] = dot(wt[...], xt[b, 0:d_model, :], ((1,), (0,)))
        arrive(g_copy(b))
        tags = gt[b].astype(F32)[0:8]
        allowed = tags[0:1, :] == tags.T[:, 0:1]
        up_all[...] = jnp.where(tags[0:1, :] < 0, gb[b].astype(F32), 0.0)
        for h in range(heads):
            o = h * 3 * HD
            query = pk[o:o + HD, :].astype(BF16)
            key = pk[o + HD:o + 2 * HD, :].astype(BF16)
            value = pk[o + 2 * HD:o + 3 * HD, :].astype(BF16)
            up = up_all[h * HD:(h + 1) * HD, :].astype(BF16)
            scores = dot(query, key, ((0,), (0,))) * scale
            masked = jnp.where(allowed, scores, -1e30)
            top = jnp.max(masked, axis=1, keepdims=True)
            exponent = jnp.where(allowed, jnp.exp(masked - top), 0.0)
            probs = exponent * (1.0 / jnp.sum(exponent, axis=1, keepdims=True))
            grad_probs = dot(up, value, ((0,), (0,)))
            row_dot = jnp.sum(probs * grad_probs, axis=1, keepdims=True)
            logits = (probs * (grad_probs - row_dot) * scale).astype(BF16)
            gps[o:o + HD, :] = dot(key, logits, ((1,), (1,)))
            gps[o + HD:o + 2 * HD, :] = dot(query, logits, ((1,), (0,)))
            gps[o + 2 * HD:o + 3 * HD, :] = dot(up, probs.astype(BF16), ((1,), (0,)))
        gp[b, rows(me * width, width), :] = gps[...].astype(BF16)
        return 0

    lax.fori_loop(0, BUNDLES, bundle, 0)
    start(p_copies(order(3)))

    def weight_block(n, _):
        total = weight_term(n, order(BUNDLES - 1))
        at = n * 2 * width
        dw[rows(at, width), :] += total[:, :LANES]
        dw[rows(at + width, width), :] += total[:, LANES:]
        return 0

    for s in range(SETS):
        lax.fori_loop(s * n_blocks // SETS, (s + 1) * n_blocks // SETS, weight_block, 0)
        core_sum(s).start()

    def add_into(at, got, got_at, size):
        dw[rows(at, size), :] += got[rows(got_at, size), :]

    def add_core(s):
        core_sum(s).wait_recv()
        add_into(s * part + core * half, c0.at[s], 0, half)

    def add_x1(s):
        arrive(x_sum1(s))
        ga, gb_ = gives(s)
        fa, fb = spans(s)[4:]
        add_into(ga, ra1.at[s], (1 - bit2) * q2, q2)
        add_into(gb_, rb1.at[s], (1 - bit1) * q2, q2)
        start(x_sum2(s))
        add_into(fa, ra1.at[s], bit2 * q2, q2)
        add_into(fb, rb1.at[s], bit1 * q2, q2)

    def loop_z(f):
        def body(k, _):
            f(k)
            return 0

        lax.fori_loop(1, nz, body, 0)

    def add_x2(s):
        arrive(x_sum2(s))
        fa, fb = spans(s)[4:]
        ze[s, 0:q2, :] = dw[rows(fa, q2), :] + ra2[s]
        ze[s, q2:2 * q2, :] = dw[rows(fb, q2), :] + rb2[s]
        start(z_half(s))

    def add_z1(s):
        arrive(z_half(s))
        zh[s, 0:q3, :] = ze[s, rows(par * q3, q3), :] + rz[s, 0:q3, :]
        zh[s, q3:2 * q3, :] = ze[s, rows(q2 + par * q3, q3), :] + rz[s, q3:2 * q3, :]
        far_copy(s).start()
        for k in direct:
            z_copy(s, k).start()

    def pass_far(s):
        far_copy(s).wait_recv()
        r = rows(((zi + 2 * last) % nz) // 2 * piece, piece)
        zh[s, r, :] += zf[s]
        z_copy(s, last).start()

    def add_z(s):
        total = zh[s, rows(zg * piece, piece), :]
        for k in direct + [last]:
            z_copy(s, k).wait_recv()
        for k in direct + [last]:
            total += zr[s, k]
        fin[rows(spot(s), piece), :] = (total * norm).astype(BF16)
        loop_z(lambda k: f_copy(s, k).start())

    def pass_on(i):
        arrive(p_copies(order(i)))
        start(p_relays(order(i)))

    def rows_grad(i):
        b = order(i)
        arrive(p_relays(b))
        gx_out[:, b * CAP:(b + 1) * CAP] = dot(wf[...], gp[b], ((1,), (0,))).astype(BF16)

    def gathered_z(s):
        loop_z(lambda k: f_copy(s, k).wait_recv())
        start(x_gather2(s))

    def gathered_x2(s):
        arrive(x_gather2(s))
        start(x_gather1(s))

    def gathered_x1(s):
        arrive(x_gather1(s))
        start(core_gather(s))

    def whole_blocks(s):
        return min(d_model // LANES, s * part // width)

    def gathered_core(s):
        arrive(core_gather(s))
        for n in range(whole_blocks(s), whole_blocks(s + 1)):
            fin_out[:, n * LANES:(n + 1) * LANES] = fin[n * width:(n + 1) * width, :]

    def early_sends_left():
        for b in range(BUNDLES):
            for cp in g_copy(b) + x_copies(b) + x_relays(b) + p_copies(b) + p_relays(b):
                cp.wait_send()
        for k in range(1, YS):
            w_copy(k).wait_send()
            v_copy(k).wait_send()
        for s in range(SETS):
            for cp in x_sum1(s) + x_sum2(s) + z_half(s) + x_gather2(s):
                cp.wait_send()
            core_sum(s).wait_send()
            far_copy(s).wait_send()
            for k in direct + [last]:
                z_copy(s, k).wait_send()
            loop_z(lambda k: f_copy(s, k).wait_send())

    def late_sends_left(sets):
        for s in sets:
            for cp in x_gather1(s) + core_gather(s):
                cp.wait_send()

    add_core(0)
    start(x_sum1(0))
    add_core(1)
    start(x_sum1(1))
    add_core(2)
    add_x1(0)
    start(x_sum1(2))
    add_x1(1)
    add_x2(0)
    add_x1(2)
    add_z1(0)
    add_x2(1)
    for k in range(1, YS):
        w_copy(k).wait_recv()
        v_copy(k).start()
    add_x2(2)
    pass_far(0)
    add_z1(1)
    add_z1(2)
    pass_on(0)
    pass_on(1)
    for k in range(1, YS):
        v_copy(k).wait_recv()
    for j in range(YS):
        wf[:, j * width:(j + 1) * width] = wfb[j]
    pass_far(1)
    add_z(0)
    pass_far(2)
    pass_on(2)
    add_z(1)
    pass_on(3)
    add_z(2)
    gathered_z(0)
    rows_grad(0)
    gathered_z(1)
    gathered_x2(0)
    rows_grad(1)
    gathered_z(2)
    gathered_x2(1)
    rows_grad(2)
    gathered_x1(0)
    gathered_x2(2)
    rows_grad(3)
    gathered_x1(1)
    gathered_core(0)
    early_sends_left()
    gathered_x1(2)
    gathered_core(1)
    late_sends_left(range(SETS - 1))
    gathered_core(2)
    late_sends_left([SETS - 1])


def shards(patches, counts, qkv_weight, grad_context):
    n_dp = lax.axis_size("dp")
    nz = n_dp // (XS * CORES)
    feat, width, grads = patches.shape[1], qkv_weight.shape[1], grad_context.shape[1]
    d_model = YS * feat
    blocks = d_model // LANES
    parts = n_dp
    unit = -(-(blocks * width) // (parts * SETS * 16)) * SETS * 16
    flat = unit * parts
    wide = 2 * LANES * (-(-blocks // 2))
    half = flat // SETS // CORES
    q1, q2 = half // 4, half // 8
    operands = patches.T, grad_context.T, qkv_weight.T, counts[0]
    dma = pltpu.SemaphoreType.DMA
    hbm_spec = pl.BlockSpec(memory_space=pltpu.HBM)
    gx, fin = pl.pallas_call(
        functools.partial(kernel, n_dp),
        out_shape=(
            jax.ShapeDtypeStruct((feat, SEQ), BF16),
            jax.ShapeDtypeStruct((width, d_model), BF16),
        ),
        in_specs=[hbm_spec] * 3 + [pl.BlockSpec(memory_space=pltpu.SMEM)],
        out_specs=(pl.BlockSpec(memory_space=pltpu.VMEM),) * 2,
        scratch_shapes=[
            pltpu.VMEM((BUNDLES, wide, CAP), BF16),
            pltpu.VMEM((width, d_model), BF16),
            pltpu.VMEM((d_model, width), BF16),
            pltpu.VMEM((BUNDLES, TAG, CAP), BF16),
            pltpu.VMEM((BUNDLES, TAG, CAP), BF16),
            pltpu.VMEM((BUNDLES, grads, CAP), BF16),
            pltpu.VMEM((width, CAP), F32),
            pltpu.VMEM((grads, CAP), F32),
            pltpu.VMEM((width, CAP), F32),
            pltpu.VMEM((BUNDLES, YS * width, CAP), BF16),
            pltpu.VMEM((YS, feat, width), BF16),
            pltpu.VMEM((feat, YS * width), BF16),
            pltpu.VMEM((max(flat, wide // LANES * width), LANES), F32),
            pltpu.VMEM((SETS, half, LANES), F32),
            pltpu.VMEM((SETS, q1, LANES), F32),
            pltpu.VMEM((SETS, q2, LANES), F32),
            pltpu.VMEM((SETS, q1, LANES), F32),
            pltpu.VMEM((SETS, q2, LANES), F32),
            pltpu.VMEM((SETS, 2 * q2, LANES), F32),
            pltpu.VMEM((SETS, q2, LANES), F32),
            pltpu.VMEM((SETS, q2, LANES), F32),
            pltpu.VMEM((SETS, 2 * q2 // nz, LANES), F32),
            pltpu.VMEM((SETS, nz // 2, 2 * q2 // nz, LANES), F32),
            pltpu.VMEM((flat, LANES), BF16),
            dma((4, BUNDLES)), dma((4, BUNDLES)),
            dma((BUNDLES,)), dma((BUNDLES,)),
            dma((BUNDLES,)), dma((BUNDLES,)),
            dma((4, BUNDLES)), dma((4, BUNDLES)),
            dma((YS - 1,)), dma((YS - 1,)),
            dma((YS - 1,)), dma((YS - 1,)),
            dma((SETS, 13)), dma((SETS, 13)),
            dma((SETS, nz // 2)), dma((SETS, nz // 2)),
            dma((SETS, nz)), dma((SETS, nz)),
            dma((BUNDLES + 1,)),
            pltpu.SemaphoreType.REGULAR((3,)),
        ],
        compiler_params=pltpu.CompilerParams(
            collective_id=0, has_side_effects=True, vmem_limit_bytes=50 * 1024 * 1024),
        name="layer",
    )(*[pltpu.with_memory_space_constraint(a, pltpu.HBM) for a in operands])
    return gx.T, fin.T


def solution(mesh):
    in_specs = (P("dp", "mp"), P("dp", None, None), P(None, "mp"), P("dp", "mp"))
    out_specs = (P("dp", "mp"), P(None, "mp"))
    return jax.shard_map(shards, mesh=mesh, in_specs=in_specs, out_specs=out_specs, check_vma=False)
```

```python
import functools
import math

import jax
import jax.numpy as jnp
from jax import lax
from jax.experimental import pallas as pl
from jax.experimental.pallas import tpu as pltpu
from jax.sharding import PartitionSpec as P

HD = 88
IMGS = 4
BUNDLES = 4
CAP = 256
SEQ = 1024
YS = 4
XS = 4
CORES = 2
LANES = 128
SETS = 3
TAG = 16

F32 = jnp.float32
BF16 = jnp.bfloat16


def dot(a, b, dims):
    return lax.dot_general(a, b, (dims, ((), ())), preferred_element_type=F32)


def kernel(
    n_dp,
    x_hbm, g_hbm, w_hbm, counts,
    gx_out, fin_out,
    xt, wt, wn, tag, gt, gb, pk, up_all, gps, gp, wfb, wf, dw, c0, ra1, ra2, rb1, rb2, ze, rz, zh, zf, zr, fin,
    x_ss, x_rs, g_ss, g_rs, t_ss, t_rs, p_ss, p_rs, w_ss, w_rs, v_ss, v_rs, d_ss, d_rs, z_ss, z_rs, f_ss, f_rs, l_sem, word,
):
    feat = x_hbm.shape[0]
    width = w_hbm.shape[0]
    heads = width // (3 * HD)
    d_model = YS * feat
    nz = n_dp // (XS * CORES)
    stride = n_dp // BUNDLES
    scale = 1.0 / math.sqrt(HD)
    norm = 1.0 / math.sqrt(n_dp)
    part = fin.shape[0] // SETS
    half = part // CORES
    sub = half // 2
    q1 = sub // 2
    q2 = q1 // 2
    q3 = q2 // 2
    piece = 2 * q2 // nz

    dp = lax.axis_index("dp")
    me = lax.axis_index("mp")
    right, left, far = (me + 1) % YS, (me + 3) % YS, (me + 2) % YS
    core = dp % CORES
    xi = (dp // CORES) % XS
    zi = dp // (XS * CORES)
    base_xz = zi * (XS * CORES)
    mate = {"dp": dp + 1 - 2 * core}
    even = xi % 2
    near1 = {"dp": base_xz + (xi + 1 - 2 * even) * CORES + core}
    near2 = {"dp": base_xz + ((xi + 3 - 2 * even) % XS) * CORES + core}
    bit1 = ((xi + 1) // 2) % 2
    bit2 = xi // 2

    par, zg = zi % 2, zi // 2
    zn1 = {"dp": dp + (1 - 2 * par) * (XS * CORES)}
    zn2 = {"dp": (dp + n_dp + (2 * par - 1) * (XS * CORES)) % n_dp}

    def z_peer(k):
        return {"dp": ((zi + k) % nz) * (XS * CORES) + xi * CORES + core}

    def remote(src, dst, ss, rs, dev):
        return pltpu.make_async_remote_copy(
            src_ref=src, dst_ref=dst, send_sem=ss, recv_sem=rs,
            device_id=dev, device_id_type=pl.DeviceIdType.MESH,
        )

    def rows(start, size):
        return pl.ds(pl.multiple_of(start, 16), size)

    def order(i):
        return (3 * i) % BUNDLES

    def cols(b):
        return pl.ds(pl.multiple_of(b * CAP, CAP), CAP)

    def g_copy(b):
        off = stride // 2 + b * stride
        to = {"dp": (dp + off) % n_dp}
        return (
            remote(tag.at[b], gt.at[b], t_ss.at[b], t_rs.at[b], to),
            remote(g_hbm.at[:, cols(b)], gb.at[b], g_ss.at[b], g_rs.at[b], to),
        )

    def x_copies(b):
        src = x_hbm.at[:, cols(b)]
        r = rows(me * feat, feat)
        return (
            remote(src, xt.at[b, r], x_ss.at[0, b], x_rs.at[0, b], {"mp": right}),
            remote(src, xt.at[b, r], x_ss.at[1, b], x_rs.at[1, b], {"mp": left}),
        )

    def x_relays(b):
        r = rows(left * feat, feat // 2)
        s = rows(right * feat + feat // 2, feat // 2)
        return (
            remote(xt.at[b, r], xt.at[b, r], x_ss.at[2, b], x_rs.at[2, b], {"mp": right}),
            remote(xt.at[b, s], xt.at[b, s], x_ss.at[3, b], x_rs.at[3, b], {"mp": left}),
        )

    def x_local(b):
        return pltpu.make_async_copy(
            x_hbm.at[:, cols(b)], xt.at[b, rows(me * feat, feat)], l_sem.at[b])

    def p_copies(b):
        r = rows(me * width, width)
        return (
            remote(gp.at[b, r], gp.at[b, r], p_ss.at[0, b], p_rs.at[0, b], {"mp": right}),
            remote(gp.at[b, r], gp.at[b, r], p_ss.at[1, b], p_rs.at[1, b], {"mp": left}),
        )

    def p_relays(b):
        r = rows(left * width, 256)
        s = rows(right * width + 256, width - 256)
        return (
            remote(gp.at[b, r], gp.at[b, r], p_ss.at[2, b], p_rs.at[2, b], {"mp": right}),
            remote(gp.at[b, s], gp.at[b, s], p_ss.at[3, b], p_rs.at[3, b], {"mp": left}),
        )

    fh = feat // CORES

    def w_copy(k):
        to = (me + k) % YS
        return remote(
            wn.at[rows(to * feat + core * fh, fh)], wfb.at[me, rows(core * fh, fh)],
            w_ss.at[k - 1], w_rs.at[k - 1], {"mp": to},
        )

    def v_copy(k):
        who = (me + YS - k) % YS
        r = rows(core * fh, fh)
        return remote(wfb.at[who, r], wfb.at[who, r], v_ss.at[k - 1], v_rs.at[k - 1], mate)

    def spans(s):
        oa = s * part + core * half
        ob = oa + sub
        keep_a, keep_b = oa + bit1 * q1, ob + bit2 * q1
        return oa, ob, keep_a, keep_b, keep_a + bit2 * q2, keep_b + bit1 * q2

    def core_sum(s):
        r = rows(s * part + (1 - core) * half, half)
        return remote(dw.at[r], c0.at[s], d_ss.at[s, 0], d_rs.at[s, 0], mate)

    def x_sum1(s):
        oa, ob = spans(s)[:2]
        ra, rb = rows(oa + (1 - bit1) * q1, q1), rows(ob + (1 - bit2) * q1, q1)
        return (
            remote(dw.at[ra], ra1.at[s], d_ss.at[s, 1], d_rs.at[s, 1], near1),
            remote(dw.at[rb], rb1.at[s], d_ss.at[s, 2], d_rs.at[s, 2], near2),
        )

    def gives(s):
        keep_a, keep_b = spans(s)[2:4]
        return keep_a + (1 - bit2) * q2, keep_b + (1 - bit1) * q2

    def x_sum2(s):
        ga, gb_ = gives(s)
        return (
            remote(dw.at[rows(ga, q2)], ra2.at[s], d_ss.at[s, 3], d_rs.at[s, 3], near2),
            remote(dw.at[rows(gb_, q2)], rb2.at[s], d_ss.at[s, 4], d_rs.at[s, 4], near1),
        )

    def z_half(s):
        give = (1 - par) * q3
        return (
            remote(ze.at[s, rows(give, q3)], rz.at[s, 0:q3], d_ss.at[s, 10], d_rs.at[s, 10], zn1),
            remote(ze.at[s, rows(q2 + give, q3)], rz.at[s, q3:2 * q3], d_ss.at[s, 11], d_rs.at[s, 11], zn2),
        )

    def z_copy(s, k):
        to = ((zi + 2 * k) % nz) // 2
        return remote(zh.at[s, rows(to * piece, piece)], zr.at[s, k], z_ss.at[s, k], z_rs.at[s, k], z_peer(2 * k))

    def far_copy(s):
        to = ((zi + nz // 2) % nz) // 2
        return remote(zh.at[s, rows(to * piece, piece)], zf.at[s], d_ss.at[s, 12], d_rs.at[s, 12], z_peer(nz - nz // 4))

    direct = [k for k in range(1, nz // 2) if k not in (nz // 4, nz // 2 - nz // 8)]
    last = nz // 2 - nz // 8

    def spot(s):
        fa, fb = spans(s)[4:]
        at = par * q3 + zg * piece
        return jnp.where(zg < nz // 4, fa + at, fb + at - q3)

    def f_copy(s, k):
        r = rows(spot(s), piece)
        return remote(fin.at[r], fin.at[r], f_ss.at[s, k], f_rs.at[s, k], z_peer(k))

    def same(s, start, size, i, dev):
        r = rows(start, size)
        return remote(fin.at[r], fin.at[r], d_ss.at[s, i], d_rs.at[s, i], dev)

    def x_gather2(s):
        fa, fb = spans(s)[4:]
        return same(s, fa, q2, 5, near2), same(s, fb, q2, 6, near1)

    def x_gather1(s):
        keep_a, keep_b = spans(s)[2:4]
        return same(s, keep_a, q1, 7, near1), same(s, keep_b, q1, 8, near2)

    def core_gather(s):
        return (same(s, s * part + core * half, half, 9, mate),)

    barrier = pltpu.get_barrier_semaphore()
    mesh_id = pl.DeviceIdType.MESH

    for dev in [{"mp": right}, {"mp": left}, mate, near1, near2, zn1, zn2]:
        pl.semaphore_signal(barrier, inc=1, device_id=dev, device_id_type=mesh_id)
    w_local = pltpu.make_async_copy(w_hbm, wt, l_sem.at[BUNDLES])
    w_local.start()
    for i in range(BUNDLES):
        x_local(order(i)).start()

    slot = lax.broadcasted_iota(jnp.int32, (TAG, CAP), 1)
    for b in range(BUNDLES):
        end = counts[b, 0]
        ids = jnp.where(slot >= end, 1, 0)
        for i in range(1, IMGS):
            end = end + counts[b, i]
            ids = ids + jnp.where(slot >= end, 1, 0)
        tag[b] = jnp.where(slot < end, ids - IMGS, slot).astype(F32).astype(BF16)
    for b in range(BUNDLES):
        xt[b, d_model:, :] = jnp.zeros((xt.shape[1] - d_model, CAP), BF16)
    pl.semaphore_wait(barrier, 7)

    def tell(i):
        for k in (2 ** i, nz - 2 ** i):
            pl.semaphore_signal(word.at[i], inc=1, device_id=z_peer(k), device_id_type=mesh_id)

    def hear(i):
        pl.semaphore_wait(word.at[i], 2)

    def start(copies):
        for cp in copies:
            cp.start()

    def arrive(copies):
        for cp in copies:
            cp.wait_recv()

    start(x_copies(0))
    start(x_copies(order(1)))
    tell(0)
    w_local.wait()
    for n in range(d_model // LANES):
        wn[n * LANES:(n + 1) * LANES, :] = wt[:, n * LANES:(n + 1) * LANES].T
    hear(0)
    tell(1)
    start(g_copy(order(0)))
    start(g_copy(order(1)))
    for i in range(BUNDLES):
        x_local(order(i)).wait()
    wfb[me] = wn[rows(me * feat, feat), :]
    hear(1)
    tell(2)

    arrive(x_copies(0))
    start(x_relays(0))
    start(x_copies(order(2)))
    hear(2)
    start(g_copy(order(2)))
    start(g_copy(order(3)))

    mine = rows(me * width, width)
    n_blocks = xt.shape[1] // (2 * LANES)

    def weight_term(n, b):
        return dot(gp[b, mine, :], xt[b, rows(n * 2 * LANES, 2 * LANES), :], ((1,), (1,)))

    def first_blocks(n, _):
        total = weight_term(n, order(0))
        for i in range(1, BUNDLES - 1):
            total += weight_term(n, order(i))
        at = n * 2 * width
        dw[rows(at, width), :] = total[:, :LANES]
        dw[rows(at + width, width), :] = total[:, LANES:]
        return 0

    def bundle(i, _):
        b = order(i)

        @pl.when(i < BUNDLES - 1)
        def _():
            nxt = order(i + 1)
            arrive(x_copies(nxt))
            start(x_relays(nxt))

        @pl.when(i == 0)
        def _():
            start(x_copies(order(3)))

        @pl.when(i == 2)
        def _():
            for k in range(1, YS):
                w_copy(k).start()
            start(p_copies(order(0)))
            start(p_copies(order(1)))

        @pl.when(i == 3)
        def _():
            start(p_copies(order(2)))
            lax.fori_loop(0, n_blocks, first_blocks, 0)

        arrive(x_relays(b))
        pk[...] = dot(wt[...], xt[b, 0:d_model, :], ((1,), (0,)))
        arrive(g_copy(b))
        tags = gt[b].astype(F32)[0:8]
        allowed = tags[0:1, :] == tags.T[:, 0:1]
        up_all[...] = jnp.where(tags[0:1, :] < 0, gb[b].astype(F32), 0.0)
        for h in range(heads):
            o = h * 3 * HD
            query = pk[o:o + HD, :].astype(BF16)
            key = pk[o + HD:o + 2 * HD, :].astype(BF16)
            value = pk[o + 2 * HD:o + 3 * HD, :].astype(BF16)
            up = up_all[h * HD:(h + 1) * HD, :].astype(BF16)
            scores = dot(query, key, ((0,), (0,))) * scale
            masked = jnp.where(allowed, scores, -1e30)
            top = jnp.max(masked, axis=1, keepdims=True)
            exponent = jnp.where(allowed, jnp.exp(masked - top), 0.0)
            probs = exponent * (1.0 / jnp.sum(exponent, axis=1, keepdims=True))
            grad_probs = dot(up, value, ((0,), (0,)))
            row_dot = jnp.sum(probs * grad_probs, axis=1, keepdims=True)
            logits = (probs * (grad_probs - row_dot) * scale).astype(BF16)
            gps[o:o + HD, :] = dot(key, logits, ((1,), (1,)))
            gps[o + HD:o + 2 * HD, :] = dot(query, logits, ((1,), (0,)))
            gps[o + 2 * HD:o + 3 * HD, :] = dot(up, probs.astype(BF16), ((1,), (0,)))
        gp[b, rows(me * width, width), :] = gps[...].astype(BF16)
        return 0

    lax.fori_loop(0, BUNDLES, bundle, 0)
    start(p_copies(order(3)))

    def weight_block(n, _):
        total = weight_term(n, order(BUNDLES - 1))
        at = n * 2 * width
        dw[rows(at, width), :] += total[:, :LANES]
        dw[rows(at + width, width), :] += total[:, LANES:]
        return 0

    for s in range(SETS):
        lax.fori_loop(s * n_blocks // SETS, (s + 1) * n_blocks // SETS, weight_block, 0)
        core_sum(s).start()

    def add_into(at, got, got_at, size):
        dw[rows(at, size), :] += got[rows(got_at, size), :]

    def add_core(s):
        core_sum(s).wait_recv()
        add_into(s * part + core * half, c0.at[s], 0, half)

    def add_x1(s):
        arrive(x_sum1(s))
        ga, gb_ = gives(s)
        fa, fb = spans(s)[4:]
        add_into(ga, ra1.at[s], (1 - bit2) * q2, q2)
        add_into(gb_, rb1.at[s], (1 - bit1) * q2, q2)
        start(x_sum2(s))
        add_into(fa, ra1.at[s], bit2 * q2, q2)
        add_into(fb, rb1.at[s], bit1 * q2, q2)

    def loop_z(f):
        def body(k, _):
            f(k)
            return 0

        lax.fori_loop(1, nz, body, 0)

    def add_x2(s):
        arrive(x_sum2(s))
        fa, fb = spans(s)[4:]
        ze[s, 0:q2, :] = dw[rows(fa, q2), :] + ra2[s]
        ze[s, q2:2 * q2, :] = dw[rows(fb, q2), :] + rb2[s]
        start(z_half(s))

    def add_z1(s):
        arrive(z_half(s))
        zh[s, 0:q3, :] = ze[s, rows(par * q3, q3), :] + rz[s, 0:q3, :]
        zh[s, q3:2 * q3, :] = ze[s, rows(q2 + par * q3, q3), :] + rz[s, q3:2 * q3, :]
        far_copy(s).start()
        for k in direct:
            z_copy(s, k).start()

    def pass_far(s):
        far_copy(s).wait_recv()
        r = rows(((zi + 2 * last) % nz) // 2 * piece, piece)
        zh[s, r, :] += zf[s]
        z_copy(s, last).start()

    def add_z(s):
        total = zh[s, rows(zg * piece, piece), :]
        for k in direct + [last]:
            z_copy(s, k).wait_recv()
        for k in direct + [last]:
            total += zr[s, k]
        fin[rows(spot(s), piece), :] = (total * norm).astype(BF16)
        loop_z(lambda k: f_copy(s, k).start())

    def pass_on(i):
        arrive(p_copies(order(i)))
        start(p_relays(order(i)))

    def rows_grad(i):
        b = order(i)
        arrive(p_relays(b))
        gx_out[:, b * CAP:(b + 1) * CAP] = dot(wf[...], gp[b], ((1,), (0,))).astype(BF16)

    def gathered_z(s):
        loop_z(lambda k: f_copy(s, k).wait_recv())
        start(x_gather2(s))

    def gathered_x2(s):
        arrive(x_gather2(s))
        start(x_gather1(s))

    def gathered_x1(s):
        arrive(x_gather1(s))
        start(core_gather(s))

    def whole_blocks(s):
        return min(d_model // LANES, s * part // width)

    def gathered_core(s):
        arrive(core_gather(s))
        for n in range(whole_blocks(s), whole_blocks(s + 1)):
            fin_out[:, n * LANES:(n + 1) * LANES] = fin[n * width:(n + 1) * width, :]

    def early_sends_left():
        for b in range(BUNDLES):
            for cp in g_copy(b) + x_copies(b) + x_relays(b) + p_copies(b) + p_relays(b):
                cp.wait_send()
        for k in range(1, YS):
            w_copy(k).wait_send()
            v_copy(k).wait_send()
        for s in range(SETS):
            for cp in x_sum1(s) + x_sum2(s) + z_half(s) + x_gather2(s):
                cp.wait_send()
            core_sum(s).wait_send()
            far_copy(s).wait_send()
            for k in direct + [last]:
                z_copy(s, k).wait_send()
            loop_z(lambda k: f_copy(s, k).wait_send())

    def late_sends_left(sets):
        for s in sets:
            for cp in x_gather1(s) + core_gather(s):
                cp.wait_send()

    add_core(0)
    start(x_sum1(0))
    add_core(1)
    start(x_sum1(1))
    add_core(2)
    add_x1(0)
    start(x_sum1(2))
    add_x1(1)
    add_x2(0)
    add_x1(2)
    add_z1(0)
    add_x2(1)
    for k in range(1, YS):
        w_copy(k).wait_recv()
        v_copy(k).start()
    add_x2(2)
    pass_far(0)
    add_z1(1)
    add_z1(2)
    pass_on(0)
    pass_on(1)
    for k in range(1, YS):
        v_copy(k).wait_recv()
    for j in range(YS):
        wf[:, j * width:(j + 1) * width] = wfb[j]
    pass_far(1)
    add_z(0)
    pass_far(2)
    add_z(1)
    pass_on(2)
    add_z(2)
    pass_on(3)
    gathered_z(0)
    gathered_z(1)
    gathered_x2(0)
    rows_grad(0)
    gathered_z(2)
    gathered_x2(1)
    rows_grad(1)
    rows_grad(2)
    gathered_x2(2)
    gathered_x1(0)
    rows_grad(3)
    gathered_x1(1)
    gathered_core(0)
    early_sends_left()
    gathered_x1(2)
    gathered_core(1)
    late_sends_left(range(SETS - 1))
    gathered_core(2)
    late_sends_left([SETS - 1])


def shards(patches, counts, qkv_weight, grad_context):
    n_dp = lax.axis_size("dp")
    nz = n_dp // (XS * CORES)
    feat, width, grads = patches.shape[1], qkv_weight.shape[1], grad_context.shape[1]
    d_model = YS * feat
    blocks = d_model // LANES
    parts = n_dp
    unit = -(-(blocks * width) // (parts * SETS * 16)) * SETS * 16
    flat = unit * parts
    wide = 2 * LANES * (-(-blocks // 2))
    half = flat // SETS // CORES
    q1, q2 = half // 4, half // 8
    operands = patches.T, grad_context.T, qkv_weight.T, counts[0]
    dma = pltpu.SemaphoreType.DMA
    hbm_spec = pl.BlockSpec(memory_space=pltpu.HBM)
    gx, fin = pl.pallas_call(
        functools.partial(kernel, n_dp),
        out_shape=(
            jax.ShapeDtypeStruct((feat, SEQ), BF16),
            jax.ShapeDtypeStruct((width, d_model), BF16),
        ),
        in_specs=[hbm_spec] * 3 + [pl.BlockSpec(memory_space=pltpu.SMEM)],
        out_specs=(pl.BlockSpec(memory_space=pltpu.VMEM),) * 2,
        scratch_shapes=[
            pltpu.VMEM((BUNDLES, wide, CAP), BF16),
            pltpu.VMEM((width, d_model), BF16),
            pltpu.VMEM((d_model, width), BF16),
            pltpu.VMEM((BUNDLES, TAG, CAP), BF16),
            pltpu.VMEM((BUNDLES, TAG, CAP), BF16),
            pltpu.VMEM((BUNDLES, grads, CAP), BF16),
            pltpu.VMEM((width, CAP), F32),
            pltpu.VMEM((grads, CAP), F32),
            pltpu.VMEM((width, CAP), F32),
            pltpu.VMEM((BUNDLES, YS * width, CAP), BF16),
            pltpu.VMEM((YS, feat, width), BF16),
            pltpu.VMEM((feat, YS * width), BF16),
            pltpu.VMEM((max(flat, wide // LANES * width), LANES), F32),
            pltpu.VMEM((SETS, half, LANES), F32),
            pltpu.VMEM((SETS, q1, LANES), F32),
            pltpu.VMEM((SETS, q2, LANES), F32),
            pltpu.VMEM((SETS, q1, LANES), F32),
            pltpu.VMEM((SETS, q2, LANES), F32),
            pltpu.VMEM((SETS, 2 * q2, LANES), F32),
            pltpu.VMEM((SETS, q2, LANES), F32),
            pltpu.VMEM((SETS, q2, LANES), F32),
            pltpu.VMEM((SETS, 2 * q2 // nz, LANES), F32),
            pltpu.VMEM((SETS, nz // 2, 2 * q2 // nz, LANES), F32),
            pltpu.VMEM((flat, LANES), BF16),
            dma((4, BUNDLES)), dma((4, BUNDLES)),
            dma((BUNDLES,)), dma((BUNDLES,)),
            dma((BUNDLES,)), dma((BUNDLES,)),
            dma((4, BUNDLES)), dma((4, BUNDLES)),
            dma((YS - 1,)), dma((YS - 1,)),
            dma((YS - 1,)), dma((YS - 1,)),
            dma((SETS, 13)), dma((SETS, 13)),
            dma((SETS, nz // 2)), dma((SETS, nz // 2)),
            dma((SETS, nz)), dma((SETS, nz)),
            dma((BUNDLES + 1,)),
            pltpu.SemaphoreType.REGULAR((3,)),
        ],
        compiler_params=pltpu.CompilerParams(
            collective_id=0, has_side_effects=True, vmem_limit_bytes=50 * 1024 * 1024),
        name="layer",
    )(*[pltpu.with_memory_space_constraint(a, pltpu.HBM) for a in operands])
    return gx.T, fin.T


def solution(mesh):
    in_specs = (P("dp", "mp"), P("dp", None, None), P(None, "mp"), P("dp", "mp"))
    out_specs = (P("dp", "mp"), P(None, "mp"))
    return jax.shard_map(shards, mesh=mesh, in_specs=in_specs, out_specs=out_specs, check_vma=False)
```
